256 devices in a mesh: rows: 64 (over z, x, core), cols: 4 (over y).
Axes of the slice: x: 4, y: 4, z: 8, core: 2. Of those that a mesh axis runs over, the one named last changes fastest.
Arguments:
- vectors: bfloat16 [1024, 262144], P(None, 'rows'), may hold values from -0.4 to 0.4
- integrals: bfloat16 [2, 256, 262144], P(None, 'cols', 'rows'), may hold values from -8 to 72
- pivots: int32 [2, 256], replicated, may hold values from 0 to 262143, as said below
Outputs:
- new_vectors: float32 [2, 256, 262144], P(None, 'cols', 'rows')
The draws below stay inside these ranges and needn't reach their ends.
Inputs may be any that keep to these rules, and one draw needn't show every extreme that they name: The 2 x 256 entries are distinct shell-pair rows. In each panel the rows of one index of rows (an aligned block of 4096) hold at most 8 pivots, and some block holds exactly 8.
All inputs are finite; a program needn't handle non-finite values.
Results may differ from the reference program's by a relative error of at most 0.00036.
Values may be sent and summed in bfloat16 or wider, within the bound.
A program may use at most 64 MiB of HBM per device.

```python
import jax
import jax.numpy as jnp

PRIOR = 1024
PW = 256
PANELS = 2
PAIR_DEV = 4096
PAIRS = 262144


group_width = 16


def pivot_lists(key):
    owners = PAIRS // PAIR_DEV
    slot_count = 2 * PW // owners
    half_count = slot_count // 2
    base = jax.random.fold_in(key, 7)
    ceiling = (2 ** 31 - 1) // PAIR_DEV - 1
    scores = jax.random.randint(jax.random.fold_in(base, 1), (owners, PAIR_DEV), 0, ceiling) * PAIR_DEV
    scores = scores + jnp.arange(PAIR_DEV, dtype=jnp.int32)[None, :]
    local_order = jnp.argsort(scores, axis=1, stable=True).astype(jnp.int32)
    offsets = jnp.zeros((owners,), jnp.int32)
    panels_out = []
    for panel in range(PANELS):
        panel_key = jax.random.fold_in(base, 100 + panel)
        swing = jax.random.randint(jax.random.fold_in(panel_key, 1), (owners // 2,), 0, half_count + 1)
        swing = swing.at[0].set(half_count)
        paired = jnp.stack([half_count + swing, half_count - swing], axis=1).reshape(-1)
        owner_scores = jax.random.randint(jax.random.fold_in(panel_key, 2), (owners,), 0, 2 ** 20) * owners
        owner_scores = owner_scores + jnp.arange(owners, dtype=jnp.int32)
        owner_order = jnp.argsort(owner_scores, stable=True).astype(jnp.int32)
        counts = jnp.zeros((owners,), jnp.int32).at[owner_order].set(paired.astype(jnp.int32))
        slots = jnp.arange(slot_count, dtype=jnp.int32)
        valid = slots[None, :] < counts[:, None]
        where = jnp.minimum(offsets[:, None] + slots[None, :], PAIR_DEV - 1)
        local_rows = jnp.take_along_axis(local_order, where, axis=1)
        global_rows = jnp.arange(owners, dtype=jnp.int32)[:, None] * PAIR_DEV + local_rows
        flat_rows = global_rows.reshape(-1)
        flat_invalid = (1 - valid.astype(jnp.int32)).reshape(-1)
        first = jnp.argsort(flat_invalid, stable=True)[:PW]
        chosen = flat_rows[first]
        shuffle_scores = jax.random.randint(jax.random.fold_in(panel_key, 3), (PW,), 0, 2 ** 20) * PW
        shuffle_scores = shuffle_scores + jnp.arange(PW, dtype=jnp.int32)
        shuffle = jnp.argsort(shuffle_scores, stable=True)
        panels_out.append(chosen[shuffle].astype(jnp.int32))
        offsets = offsets + counts
    return jnp.stack(panels_out)


def draw_pivots(key, part):
    return pivot_lists(key)


def draw_vectors(key, part):
    base_key = jax.random.fold_in(key, 21)
    factor = 2.0 * PRIOR ** (-0.5)
    values = jnp.clip(jax.random.normal(jax.random.fold_in(base_key, 5), (PRIOR, PAIRS), jnp.float32), -6.0, 6.0)
    return jnp.clip(values * factor, -0.3984375, 0.3984375).astype(jnp.bfloat16)


def draw_integrals(key, part):
    pivot_table = pivot_lists(key)
    noise_key = jax.random.fold_in(key, 11)
    noise = jnp.clip(jax.random.normal(noise_key, (PANELS, PW, PAIRS), jnp.float32), -6.0, 6.0)
    group_count = (PW + group_width - 1) // group_width
    strength = jax.random.uniform(jax.random.fold_in(key, 13), (PANELS, group_count), jnp.float32, 24.0, 40.0)
    position = jnp.arange(PW, dtype=jnp.int32)
    member = position // group_width
    same_group = (member[:, None] == member[None, :]).astype(jnp.float32)
    identity = (position[:, None] == position[None, :]).astype(jnp.float32)
    coupling = jnp.take(strength, member, axis=1)[:, :, None] * (same_group * (1.0 - identity))[None, :, :]
    pattern = 64.0 * identity[None, :, :] + coupling
    panel_index = jnp.arange(PANELS, dtype=jnp.int32)[:, None, None]
    row_index = position[None, :, None]
    column_index = pivot_table[:, None, :]
    structure = jnp.zeros((PANELS, PW, PAIRS), jnp.float32).at[panel_index, row_index, column_index].set(pattern)
    column_scale = jnp.ones((PAIRS,), jnp.float32).at[pivot_table.reshape(-1)].set(0.125)
    return (noise * column_scale[None, None, :] + structure).astype(jnp.bfloat16)


def setup_inputs(seed: int = 0) -> dict:
    streams_of = jax.random.split(jax.random.key(seed), 4)
    return {
        "vectors": draw_vectors(jax.random.fold_in(streams_of[3], 71), 0),
        "integrals": draw_integrals(jax.random.fold_in(streams_of[3], 71), 0),
        "pivots": draw_pivots(jax.random.fold_in(streams_of[3], 71), 0),
    }


def factor_panel(residual, pivot_row):
    block = jnp.take(residual, pivot_row, axis=1)
    symmetric = 0.5 * (block + block.T)
    lower_factor = jnp.linalg.cholesky(symmetric)
    return jax.scipy.linalg.solve_triangular(lower_factor, residual, lower=True)

def reference(vectors, integrals, pivots):
    factors = [vectors]
    results = []
    for panel in range(PANELS):
        pivot_row = pivots[panel].astype(jnp.int32)
        residual = integrals[panel].astype(jnp.float32)
        for factor in factors:
            chosen = jnp.take(factor, pivot_row, axis=1).T
            residual = residual - jnp.dot(chosen.astype(jnp.float32), factor.astype(jnp.float32), preferred_element_type=jnp.float32)
        fresh = factor_panel(residual, pivot_row)
        results.append(fresh)
        factors.append(fresh.astype(jnp.bfloat16))
    return jnp.stack(results)
```

```python
import functools

import jax
import jax.numpy as jnp
from jax import lax
from jax.experimental import pallas as pl
from jax.experimental.pallas import tpu as pltpu
from jax.sharding import Mesh
from jax.sharding import PartitionSpec as P

PW = 256
PANELS = 2
SLOTS = 8
ROWS = ("rows_0", "rows_1", "rows_2")
HI = lax.Precision.HIGHEST

def bsub(x, k):
    return jnp.broadcast_to(x[k:k+1, :], (8, 128))

def blane(x, k):
    return jnp.broadcast_to(x[:, k:k+1], (8, 128))

def factor_inverse_128(rows):
    sub = lax.broadcasted_iota(jnp.int32, (8, 128), 0)
    lane = lax.broadcasted_iota(jnp.int32, (8, 128), 1)
    out = []
    for s in range(16):
        base = 8 * s
        r = rows[s]
        cols = [blane(r, base + k) for k in range(8)]
        a = {}
        for k in range(8):
            for i in range(k, 8):
                a[i, k] = bsub(cols[k], i)
        unit, pivot = [], []
        for k in range(8):
            g = lambda i, j: a[max(i, j), min(i, j)]
            d = a[k, k]
            pivot.append(d)
            unit.append([g(k, j) for j in range(k)])
            p = 1.0 / d
            others = [i for i in range(8) if i != k]
            b = {i: g(i, k) * p for i in others}
            new = dict(a)
            for x, i in enumerate(others):
                for j in others[:x + 1]:
                    new[i, j] = a[i, j] - b[i] * g(j, k)
                new[max(i, k), min(i, k)] = b[i]
            new[k, k] = -p
            a = new
        def column(vals):
            v = vals[0]
            for i in range(1, 8):
                v = jnp.where(sub == i, vals[i], v)
            return v
        g = lambda i, j: a[max(i, j), min(i, j)]
        ninv = [column([g(i, k) for i in range(8)]) for k in range(8)]
        scale = lax.rsqrt(column(pivot))
        kcol = []
        for j in range(8):
            v = jnp.where(sub == j, scale, 0.0)
            for i in range(j + 1, 8):
                v = jnp.where(sub == i, -unit[i][j] * scale, v)
            kcol.append(v)
        inblock = (lane >= base) & (lane < base + 8)
        rp = jnp.where(inblock, jnp.where(lane - base == sub, 1.0, 0.0), r)
        brow = [bsub(rp, k) for k in range(8)]
        fin = kcol[0] * brow[0]
        for k in range(1, 8):
            fin = fin + kcol[k] * brow[k]
        out.append(jnp.where(lane < base + 8, fin, 0.0))
        if s == 15:
            break
        ny = ninv[0] * brow[0]
        for k in range(1, 8):
            ny = ny + ninv[k] * brow[k]
        yb = [bsub(ny, k) for k in range(8)]
        for t in range(s + 1, 16):
            rt = rows[t]
            c = [blane(rt, base + k) for k in range(8)]
            acc0 = c[0] * yb[0]
            acc1 = c[1] * yb[1]
            for k in range(2, 8, 2):
                acc0 = acc0 + c[k] * yb[k]
                acc1 = acc1 + c[k + 1] * yb[k + 1]
            rows[t] = jnp.where(inblock, 0.0, rt) + (acc0 + acc1)
    return out

def nt(a, b, precision=HI):
    return lax.dot_general(a, b, (((1,), (1,)), ((), ())), precision=precision, preferred_element_type=jnp.float32)

def nn(a, b, precision=HI):
    return lax.dot_general(a, b, (((1,), (0,)), ((), ())), precision=precision, preferred_element_type=jnp.float32)

def inverse_factor(a_ref, l_ref):
    half = lambda ref, r, c: ref[pl.ds(128 * r, 128), pl.ds(128 * c, 128)]
    w = factor_inverse_128([a_ref[pl.ds(8 * i, 8), pl.ds(0, 128)] for i in range(16)])
    for i in range(16):
        l_ref[pl.ds(8 * i, 8), pl.ds(0, 128)] = w[i]
    l11 = half(l_ref, 0, 0)
    t21 = nt(half(a_ref, 1, 0), l11)
    a_ref[pl.ds(128, 128), pl.ds(128, 128)] = half(a_ref, 1, 1) - nt(t21, t21)
    w = factor_inverse_128([a_ref[pl.ds(128 + 8 * i, 8), pl.ds(128, 128)] for i in range(16)])
    for i in range(16):
        l_ref[pl.ds(128 + 8 * i, 8), pl.ds(128, 128)] = w[i]
    l22 = half(l_ref, 1, 1)
    l_ref[pl.ds(128, 128), pl.ds(0, 128)] = -nn(l22, nn(t21, l11))
    l_ref[pl.ds(0, 128), pl.ds(128, 128)] = jnp.zeros((128, 128), jnp.float32)

def one_pass_nt(a, b):
    return nt(a, b, None)


def split(x):
    high = x.astype(jnp.bfloat16)
    return high, (x - high.astype(jnp.float32)).astype(jnp.bfloat16)


def factor_kernel(g_ref, slot_ref, gt_ref, l0_ref, l1_ref, ft_ref, i0_ref, i1_ref, a_ref, l_ref):
    rows = g_ref.shape[1]
    pick = (lax.broadcasted_iota(jnp.int32, (2 * PW, rows), 1) == slot_ref[...]).astype(jnp.bfloat16)
    parts = g_ref.shape[0]
    depth = gt_ref.shape[1] // parts
    width = PW // parts
    for y in range(parts):
        t = nn(pick, g_ref[y], None)
        gt_ref[:, pl.ds(depth * y, depth)] = t[:, :depth].astype(jnp.bfloat16)
        i0_ref[:, pl.ds(width * y, width)] = t[:, depth : depth + width]
        i1_ref[:, pl.ds(width * y, width)] = t[PW:, depth + width :]
    g0, g1 = gt_ref[pl.ds(0, PW), :], gt_ref[pl.ds(PW, PW), :]
    own = i0_ref[pl.ds(0, PW), :]
    a_ref[...] = 0.5 * (own + own.T) - one_pass_nt(g0, g0)
    inverse_factor(a_ref, l_ref)
    l0 = l_ref[...]
    high, low = split(l0)
    l0_ref[pl.ds(0, PW), :] = high
    l0_ref[pl.ds(PW, PW), :] = low
    later = i0_ref[pl.ds(PW, PW), :] - one_pass_nt(g1, g0)
    ft = nt(later, l0).astype(jnp.bfloat16)
    ft_ref[...] = ft
    own = i1_ref[...]
    a_ref[...] = 0.5 * (own + own.T) - one_pass_nt(g1, g1) - one_pass_nt(ft, ft)
    inverse_factor(a_ref, l_ref)
    high, low = split(l_ref[...])
    l1_ref[pl.ds(0, PW), :] = high
    l1_ref[pl.ds(PW, PW), :] = low


def factor(gathered, slot_of):
    depth = 1024
    full = lambda shape, dtype: jax.ShapeDtypeStruct(shape, dtype)
    return pl.pallas_call(
        factor_kernel,
        out_shape=(
            full((2 * PW, depth), jnp.bfloat16),
            full((2 * PW, PW), jnp.bfloat16),
            full((2 * PW, PW), jnp.bfloat16),
            full((PW, PW), jnp.bfloat16),
        ),
        scratch_shapes=[
            pltpu.VMEM((2 * PW, PW), jnp.float32),
            pltpu.VMEM((PW, PW), jnp.float32),
            pltpu.VMEM((PW, PW), jnp.float32),
            pltpu.VMEM((PW, PW), jnp.float32),
        ],
        compiler_params=pltpu.CompilerParams(vmem_limit_bytes=40 << 20),
        cost_estimate=pl.CostEstimate(flops=10**9, bytes_accessed=6 << 20, transcendentals=0),
        name="factor",
    )(gathered, slot_of)


def apply_kernel(v_ref, own_ref, left_ref, right_ref, far_ref, gt_ref, l0_ref, l1_ref, ft_ref, out_ref, r_ref):
    me = lax.axis_index("cols")
    width = own_ref.shape[1]
    shards = (own_ref, right_ref, far_ref, left_ref)

    def residual(panel):
        r_ref[...] = -nn(gt_ref[pl.ds(PW * panel, PW), :], v_ref[...], None)
        for k, shard in enumerate(shards):
            at = pl.ds(pl.multiple_of(lax.rem(me + k, 4) * width, width), width)
            r_ref[at, :] += shard[panel].astype(jnp.float32)

    mine = pl.multiple_of(me * width, width)
    residual(0)
    high, low = split(r_ref[...])
    both = nn(l0_ref[...], high, None)
    x = both[:PW] + both[PW:] + nn(l0_ref[pl.ds(0, PW), :], low, None)
    rounded = x.astype(jnp.bfloat16)
    r_ref[...] = x
    out_ref[0] = r_ref[pl.ds(mine, width), :]
    residual(1)
    r = r_ref[...] - lax.dot_general(ft_ref[...], rounded, (((1,), (0,)), ((), ())), preferred_element_type=jnp.float32)
    high, low = split(r)
    lh = l1_ref[pl.ds(mine, width), :]
    ll = l1_ref[pl.ds(pl.multiple_of(PW + mine, width), width), :]
    out_ref[1] = nn(lh, high, None) + (nn(ll, high, None) + nn(lh, low, None))


def apply_factors(vectors, shards, gt, l0, l1, ft):
    depth, columns = vectors.shape
    width = shards[0].shape[1]
    chunk = 512
    whole = lambda x: pl.BlockSpec(x.shape, lambda j: (0,) * x.ndim, pipeline_mode=pl.Buffered(1))
    part = pl.BlockSpec((PANELS, width, chunk), lambda j: (0, 0, j))
    return pl.pallas_call(
        apply_kernel,
        grid=(columns // chunk,),
        in_specs=[pl.BlockSpec((depth, chunk), lambda j: (0, j))] + [part] * 4 + [whole(x) for x in (gt, l0, l1, ft)],
        out_specs=part,
        out_shape=jax.ShapeDtypeStruct((PANELS, width, columns), jnp.float32),
        scratch_shapes=[pltpu.VMEM((PW, chunk), jnp.float32)],
        compiler_params=pltpu.CompilerParams(vmem_limit_bytes=40 << 20),
        cost_estimate=pl.CostEstimate(flops=7 * 10**9, bytes_accessed=16 << 20, transcendentals=0),
        name="apply",
    )(vectors, *shards, gt, l0, l1, ft)


def neighbours(integrals):
    size = 4
    hop = lambda x, by: lax.ppermute(x, "cols", [(i, (i + by) % size) for i in range(size)])
    right = hop(integrals, -1)
    left = hop(integrals, 1)
    half = integrals.shape[2] // 2
    far = jnp.concatenate([hop(left[:, :, :half], 1), hop(right[:, :, half:], -1)], axis=2)
    return right, far, left


def slots(pivots, row_count):
    owner = pivots // row_count
    order = jnp.arange(PW, dtype=jnp.int32)
    earlier = (owner[:, None, :] == owner[:, :, None]) & (order[None, None, :] < order[None, :, None])
    rank = jnp.sum(earlier.astype(jnp.int32), axis=2)
    panel = jnp.arange(PANELS, dtype=jnp.int32)[:, None]
    return (owner * PANELS + panel) * SLOTS + rank


def per_device(vectors, integrals, pivots):
    row_count = vectors.shape[1]
    width = integrals.shape[1]
    owners = lax.axis_size(ROWS)
    parts = lax.axis_size("cols")
    depth = vectors.shape[0] // parts
    me = lax.axis_index(ROWS)
    col = lax.axis_index("cols")
    right, far, left = neighbours(integrals)
    slot_of = slots(pivots, row_count).reshape(-1)
    mine = me * PANELS * SLOTS + jnp.arange(PANELS * SLOTS, dtype=jnp.int32)
    local = pivots.reshape(-1) - me * row_count
    hit = slot_of[None, :] == mine[:, None]
    place = jnp.sum(jnp.where(hit, local[None, :] + 1, 0), axis=1) - 1
    pick = (place[:, None] == jnp.arange(row_count, dtype=jnp.int32)[None, :]).astype(jnp.bfloat16)
    share = lax.dynamic_slice_in_dim(vectors, col * depth, depth, 0)
    take = lambda x: nt(pick, x, None).astype(jnp.bfloat16)
    sending = jnp.concatenate([take(share), take(integrals[0]), take(integrals[1])], axis=1)
    gathered = lax.all_gather(sending, ("cols", *ROWS), tiled=True)
    gathered = gathered.reshape(parts, owners * PANELS * SLOTS, -1)
    gt, l0, l1, ft = factor(gathered, slot_of[:, None])
    return apply_factors(vectors, (integrals, left, right, far), gt, l0, l1, ft)


def solution(mesh):
    torus = Mesh(
        mesh.devices.reshape(8, 4, 2, mesh.shape["cols"]), ("rows_0", "rows_1", "rows_2", "cols")
    )
    return jax.shard_map(
        per_device,
        mesh=torus,
        in_specs=(P(None, ROWS), P(None, "cols", ROWS), P()),
        out_specs=P(None, "cols", ROWS),
        check_vma=False,
    )
```

```python
import functools

import jax
import jax.numpy as jnp
from jax import lax
from jax.experimental import pallas as pl
from jax.experimental.pallas import tpu as pltpu
from jax.sharding import Mesh
from jax.sharding import PartitionSpec as P

PW = 256
PANELS = 2
SLOTS = 8
ROWS = ("rows_0", "rows_1", "rows_2")
HI = lax.Precision.HIGHEST
MESH = pl.DeviceIdType.MESH


def bsub(x, k):
    return jnp.broadcast_to(x[k:k+1, :], (8, 128))

def blane(x, k):
    return jnp.broadcast_to(x[:, k:k+1], (8, 128))

def factor_inverse_128(rows):
    sub = lax.broadcasted_iota(jnp.int32, (8, 128), 0)
    lane = lax.broadcasted_iota(jnp.int32, (8, 128), 1)
    out = []
    for s in range(16):
        base = 8 * s
        r = rows[s]
        cols = [blane(r, base + k) for k in range(8)]
        a = {}
        for k in range(8):
            for i in range(k, 8):
                a[i, k] = bsub(cols[k], i)
        unit, pivot = [], []
        for k in range(8):
            g = lambda i, j: a[max(i, j), min(i, j)]
            d = a[k, k]
            pivot.append(d)
            unit.append([g(k, j) for j in range(k)])
            p = 1.0 / d
            others = [i for i in range(8) if i != k]
            b = {i: g(i, k) * p for i in others}
            new = dict(a)
            for x, i in enumerate(others):
                for j in others[:x + 1]:
                    new[i, j] = a[i, j] - b[i] * g(j, k)
                new[max(i, k), min(i, k)] = b[i]
            new[k, k] = -p
            a = new
        def column(vals):
            v = vals[0]
            for i in range(1, 8):
                v = jnp.where(sub == i, vals[i], v)
            return v
        g = lambda i, j: a[max(i, j), min(i, j)]
        ninv = [column([g(i, k) for i in range(8)]) for k in range(8)]
        scale = lax.rsqrt(column(pivot))
        kcol = []
        for j in range(8):
            v = jnp.where(sub == j, scale, 0.0)
            for i in range(j + 1, 8):
                v = jnp.where(sub == i, -unit[i][j] * scale, v)
            kcol.append(v)
        inblock = (lane >= base) & (lane < base + 8)
        rp = jnp.where(inblock, jnp.where(lane - base == sub, 1.0, 0.0), r)
        brow = [bsub(rp, k) for k in range(8)]
        fin = kcol[0] * brow[0]
        for k in range(1, 8):
            fin = fin + kcol[k] * brow[k]
        out.append(jnp.where(lane < base + 8, fin, 0.0))
        if s == 15:
            break
        ny = ninv[0] * brow[0]
        for k in range(1, 8):
            ny = ny + ninv[k] * brow[k]
        yb = [bsub(ny, k) for k in range(8)]
        for t in range(s + 1, 16):
            rt = rows[t]
            c = [blane(rt, base + k) for k in range(8)]
            acc0 = c[0] * yb[0]
            acc1 = c[1] * yb[1]
            for k in range(2, 8, 2):
                acc0 = acc0 + c[k] * yb[k]
                acc1 = acc1 + c[k + 1] * yb[k + 1]
            rows[t] = jnp.where(inblock, 0.0, rt) + (acc0 + acc1)
    return out

def nt(a, b, precision=HI):
    return lax.dot_general(a, b, (((1,), (1,)), ((), ())), precision=precision, preferred_element_type=jnp.float32)

def nn(a, b, precision=HI):
    return lax.dot_general(a, b, (((1,), (0,)), ((), ())), precision=precision, preferred_element_type=jnp.float32)

def inverse_factor(a_ref, l_ref):
    half = lambda ref, r, c: ref[pl.ds(128 * r, 128), pl.ds(128 * c, 128)]
    w = factor_inverse_128([a_ref[pl.ds(8 * i, 8), pl.ds(0, 128)] for i in range(16)])
    for i in range(16):
        l_ref[pl.ds(8 * i, 8), pl.ds(0, 128)] = w[i]
    l11 = half(l_ref, 0, 0)
    t21 = nt(half(a_ref, 1, 0), l11)
    a_ref[pl.ds(128, 128), pl.ds(128, 128)] = half(a_ref, 1, 1) - nt(t21, t21)
    w = factor_inverse_128([a_ref[pl.ds(128 + 8 * i, 8), pl.ds(128, 128)] for i in range(16)])
    for i in range(16):
        l_ref[pl.ds(128 + 8 * i, 8), pl.ds(128, 128)] = w[i]
    l22 = half(l_ref, 1, 1)
    l_ref[pl.ds(128, 128), pl.ds(0, 128)] = -nn(l22, nn(t21, l11))
    l_ref[pl.ds(0, 128), pl.ds(128, 128)] = jnp.zeros((128, 128), jnp.float32)

def gather_kernel(own_ref, out_ref, send_sem, recv_sem, local_sem):
    parts, deep, wide = out_ref.shape[:3]
    half = out_ref.shape[3] // 2
    z, x, c, y = (lax.axis_index(axis) for axis in (*ROWS, "cols"))
    first, second = 2 * c, 2 * c + 1
    handler = y // 2
    slot = [16]
    started = []

    barrier = pltpu.get_barrier_semaphore()
    greeted = 0
    for other in range(1, 2 * parts):
        where = lax.rem(2 * y + c + other, 2 * parts)
        pl.semaphore_signal(barrier, device_id={"cols": where // 2, "rows_2": lax.rem(where, 2)}, device_id_type=MESH)
        greeted += 1
    for other in range(1, wide):
        pl.semaphore_signal(barrier, device_id={"rows_1": lax.rem(x + other, wide)}, device_id_type=MESH)
        greeted += 1
    for other in (1, deep - 1):
        pl.semaphore_signal(barrier, device_id={"rows_0": lax.rem(z + other, deep)}, device_id_type=MESH)
        greeted += 1
    pl.semaphore_wait(barrier, greeted)

    def send(src, to, dst=None):
        i = slot[0]
        slot[0] += 1
        copy = pltpu.make_async_remote_copy(
            src_ref=src, dst_ref=src, send_sem=send_sem.at[i], recv_sem=recv_sem.at[i], device_id=to, device_id_type=MESH
        )
        copy.start()
        started.append(copy)
        return copy

    mine = out_ref.at[y, z, x, pl.ds(half * c, half)]
    local = pltpu.make_async_copy(own_ref, mine, local_sem)
    here = handler == c

    def own_copy(t):
        return pltpu.make_async_remote_copy(
            src_ref=own_ref,
            dst_ref=mine,
            send_sem=send_sem.at[t],
            recv_sem=recv_sem.at[lax.rem(y, 2) * 2 + c],
            device_id={"cols": t, "rows_2": handler},
            device_id_type=MESH,
        )

    away = []
    for other in range(parts):
        t = lax.rem(y + other, parts)
        go = here if other == 0 else None
        if other == 0:
            pl.when(jnp.logical_not(here))(lambda t=t: own_copy(t).start())
        else:
            own_copy(t).start()
        away.append(t)
    pl.when(here)(lambda: local.start())
    pl.when(here)(lambda: local.wait())

    def arrived(p):
        for k in range(2):
            block = out_ref.at[2 * c + p, z, x, pl.ds(half * k, half)]
            copy = pltpu.make_async_remote_copy(
                src_ref=block, dst_ref=block, send_sem=send_sem.at[0], recv_sem=recv_sem.at[2 * p + k],
                device_id={"cols": y, "rows_2": 1 - c}, device_id_type=MESH,
            )
            pl.when(jnp.logical_or(2 * c + p != y, c != k))(lambda copy=copy: copy.wait_recv())

    up, down = {"rows_0": lax.rem(z + 1, deep)}, {"rows_0": lax.rem(z + deep - 1, deep)}
    right, left = {"rows_1": lax.rem(x + 1, wide)}, {"rows_1": lax.rem(x + wide - 1, wide)}
    sibling = {"rows_2": 1 - c}
    at_z = lambda k: lax.rem(z + k + deep, deep)
    at_x = lambda k: lax.rem(x + k + wide, wide)
    last = deep // 2 - 1

    def ring(part, step):
        a, b = part(at_z(-step)), part(at_z(step))
        if step == last:
            size = a.shape[0] // 2
            a, b = a.at[pl.ds(0, size)], b.at[pl.ds(size, size)]
        return send(a, up), send(b, down)

    slab = lambda k: out_ref.at[first, k]
    piece = lambda k: out_ref.at[second, k, x]
    across = []
    to_sibling = []

    def spread(k):
        p = piece(at_z(k))
        across.append((k, send(p, right), send(p, left)))

    arrived(1)
    ring_b = ring(piece, 0)
    spread(0)
    arrived(0)
    block = out_ref.at[first, z, x]
    near = [send(block, {"rows_1": at_x(k)}) for k in (1, 3, 2)]

    def step_b(step):
        nonlocal ring_b
        for copy in ring_b:
            copy.wait_recv()
        if step < last:
            ring_b = ring(piece, step + 1)
            spread(-step - 1)
            spread(step + 1)
        else:
            spread(step + 1)

    def step_a(step):
        nonlocal ring_a
        for copy in ring_a:
            copy.wait_recv()
        if step < last:
            ring_a = ring(slab, step + 1)
            to_sibling.append(send(slab(at_z(-step - 1)), sibling))
        to_sibling.append(send(slab(at_z(step + 1)), sibling))

    for copy in near:
        copy.wait_recv()
    ring_a = ring(slab, 0)
    to_sibling.append(send(slab(z), sibling))
    step_b(0)
    step_b(1)
    step_a(0)
    step_b(2)
    step_b(3)
    to_sibling.append(send(out_ref.at[second, :, x], sibling))
    step_a(1)
    onward = []
    for n, (k, a, b) in enumerate(across):
        a.wait_recv()
        b.wait_recv()
        if n % 2 == 0:
            onward.append(send(out_ref.at[second, at_z(k), at_x(-1)], right))
        else:
            onward.append(send(out_ref.at[second, at_z(k), at_x(1)], left))
    to_sibling.append(send(out_ref.at[second, :, at_x(1)], sibling))
    to_sibling.append(send(out_ref.at[second, :, at_x(-1)], sibling))
    step_a(2)
    for copy in onward:
        copy.wait_recv()
    to_sibling.append(send(out_ref.at[second, :, at_x(2)], sibling))
    step_a(3)
    for copy in to_sibling:
        copy.wait_recv()
    for copy in started:
        copy.wait_send()
    for other, t in enumerate(away):
        if other == 0:
            pl.when(jnp.logical_not(here))(lambda t=t: own_copy(t).wait_send())
        else:
            own_copy(t).wait_send()


def gather_slots(own, owners, parts):
    lines, width = own.shape
    deep, wide = lax.axis_size(ROWS[0]), lax.axis_size(ROWS[1])
    count = 96
    return pl.pallas_call(
        gather_kernel,
        out_shape=jax.ShapeDtypeStruct((parts, deep, wide, 2 * lines, width), own.dtype),
        in_specs=[pl.BlockSpec(memory_space=pl.ANY)],
        out_specs=pl.BlockSpec(memory_space=pl.ANY),
        scratch_shapes=[pltpu.SemaphoreType.DMA((count,)), pltpu.SemaphoreType.DMA((count,)), pltpu.SemaphoreType.DMA],
        compiler_params=pltpu.CompilerParams(collective_id=0, has_side_effects=True),
        cost_estimate=pl.CostEstimate(flops=0, bytes_accessed=40 << 20, transcendentals=0),
        name="gather_slots",
    )(own).reshape(parts, owners * lines, width)


def one_pass_nt(a, b):
    return nt(a, b, None)


def split(x):
    high = x.astype(jnp.bfloat16)
    return high, (x - high.astype(jnp.float32)).astype(jnp.bfloat16)


def factor_kernel(g_ref, slot_ref, gt_ref, l0_ref, l1_ref, ft_ref, i0_ref, i1_ref, a_ref, l_ref):
    rows = g_ref.shape[1]
    pick = (lax.broadcasted_iota(jnp.int32, (2 * PW, rows), 1) == slot_ref[...]).astype(jnp.bfloat16)
    parts = g_ref.shape[0]
    depth = gt_ref.shape[1] // parts
    width = PW // parts
    for y in range(parts):
        t = nn(pick, g_ref[y], None)
        gt_ref[:, pl.ds(depth * y, depth)] = t[:, :depth].astype(jnp.bfloat16)
        i0_ref[:, pl.ds(width * y, width)] = t[:, depth : depth + width]
        i1_ref[:, pl.ds(width * y, width)] = t[PW:, depth + width :]
    g0, g1 = gt_ref[pl.ds(0, PW), :], gt_ref[pl.ds(PW, PW), :]
    own = i0_ref[pl.ds(0, PW), :]
    a_ref[...] = 0.5 * (own + own.T) - one_pass_nt(g0, g0)
    inverse_factor(a_ref, l_ref)
    l0 = l_ref[...]
    high, low = split(l0)
    l0_ref[pl.ds(0, PW), :] = high
    l0_ref[pl.ds(PW, PW), :] = low
    later = i0_ref[pl.ds(PW, PW), :] - one_pass_nt(g1, g0)
    ft = nt(later, l0).astype(jnp.bfloat16)
    ft_ref[...] = ft
    own = i1_ref[...]
    a_ref[...] = 0.5 * (own + own.T) - one_pass_nt(g1, g1) - one_pass_nt(ft, ft)
    inverse_factor(a_ref, l_ref)
    high, low = split(l_ref[...])
    l1_ref[pl.ds(0, PW), :] = high
    l1_ref[pl.ds(PW, PW), :] = low


def factor(gathered, slot_of):
    depth = 1024
    full = lambda shape, dtype: jax.ShapeDtypeStruct(shape, dtype)
    return pl.pallas_call(
        factor_kernel,
        out_shape=(
            full((2 * PW, depth), jnp.bfloat16),
            full((2 * PW, PW), jnp.bfloat16),
            full((2 * PW, PW), jnp.bfloat16),
            full((PW, PW), jnp.bfloat16),
        ),
        scratch_shapes=[
            pltpu.VMEM((2 * PW, PW), jnp.float32),
            pltpu.VMEM((PW, PW), jnp.float32),
            pltpu.VMEM((PW, PW), jnp.float32),
            pltpu.VMEM((PW, PW), jnp.float32),
        ],
        compiler_params=pltpu.CompilerParams(vmem_limit_bytes=40 << 20),
        cost_estimate=pl.CostEstimate(flops=10**9, bytes_accessed=6 << 20, transcendentals=0),
        name="factor",
    )(gathered, slot_of)


def apply_kernel(v_ref, own_ref, *refs):
    shards, (gt_ref, l0_ref, l1_ref, ft_ref, out_ref, r_ref) = refs[:6], refs[6:]
    me = lax.axis_index("cols")
    width = own_ref.shape[1]

    def residual(panel):
        r_ref[...] = -nn(gt_ref[pl.ds(PW * panel, PW), :], v_ref[...], None)
        for k in range(4):
            at = pl.ds(pl.multiple_of(lax.rem(me + k, 4) * width, width), width)
            shard = own_ref[panel] if k == 0 else shards[3 * panel + k - 1][...]
            r_ref[at, :] += shard.astype(jnp.float32)

    mine = pl.multiple_of(me * width, width)
    residual(0)
    high, low = split(r_ref[...])
    both = nn(l0_ref[...], high, None)
    x = both[:PW] + both[PW:] + nn(l0_ref[pl.ds(0, PW), :], low, None)
    rounded = x.astype(jnp.bfloat16)
    r_ref[...] = x
    out_ref[0] = r_ref[pl.ds(mine, width), :]
    residual(1)
    r = r_ref[...] - lax.dot_general(ft_ref[...], rounded, (((1,), (0,)), ((), ())), preferred_element_type=jnp.float32)
    high, low = split(r)
    lh = l1_ref[pl.ds(mine, width), :]
    ll = l1_ref[pl.ds(pl.multiple_of(PW + mine, width), width), :]
    out_ref[1] = nn(lh, high, None) + (nn(ll, high, None) + nn(lh, low, None))


def apply_factors(vectors, integrals, shards, gt, l0, l1, ft):
    depth, columns = vectors.shape
    width = integrals.shape[1]
    chunk = 512
    whole = lambda x: pl.BlockSpec(x.shape, lambda j: (0,) * x.ndim, pipeline_mode=pl.Buffered(1))
    part = pl.BlockSpec((PANELS, width, chunk), lambda j: (0, 0, j))
    one = pl.BlockSpec((width, chunk), lambda j: (0, j))
    return pl.pallas_call(
        apply_kernel,
        grid=(columns // chunk,),
        in_specs=[pl.BlockSpec((depth, chunk), lambda j: (0, j))] + [part] + [one] * 6 + [whole(x) for x in (gt, l0, l1, ft)],
        out_specs=part,
        out_shape=jax.ShapeDtypeStruct((PANELS, width, columns), jnp.float32),
        scratch_shapes=[pltpu.VMEM((PW, chunk), jnp.float32)],
        compiler_params=pltpu.CompilerParams(vmem_limit_bytes=40 << 20),
        cost_estimate=pl.CostEstimate(flops=7 * 10**9, bytes_accessed=16 << 20, transcendentals=0),
        name="apply",
    )(vectors, integrals, *shards, gt, l0, l1, ft)


def hop(x, by):
    size = lax.axis_size("cols")
    return lax.ppermute(x, "cols", [(i, (i + by) % size) for i in range(size)])


def slots(pivots, row_count):
    owner = pivots // row_count
    order = jnp.arange(PW, dtype=jnp.int32)
    earlier = (owner[:, None, :] == owner[:, :, None]) & (order[None, None, :] < order[None, :, None])
    rank = jnp.sum(earlier.astype(jnp.int32), axis=2)
    panel = jnp.arange(PANELS, dtype=jnp.int32)[:, None]
    return (owner * PANELS + panel) * SLOTS + rank


def per_device(vectors, integrals, pivots):
    row_count = vectors.shape[1]
    width = integrals.shape[1]
    owners = lax.axis_size(ROWS)
    parts = lax.axis_size("cols")
    depth = vectors.shape[0] // parts
    me = lax.axis_index(ROWS)
    col = lax.axis_index("cols")
    right = [hop(integrals[p], -1) for p in range(PANELS)]
    left = [hop(integrals[p], 1) for p in range(PANELS)]
    slot_of = slots(pivots, row_count).reshape(-1)
    mine = me * PANELS * SLOTS + jnp.arange(PANELS * SLOTS, dtype=jnp.int32)
    local = pivots.reshape(-1) - me * row_count
    hit = slot_of[None, :] == mine[:, None]
    place = jnp.sum(jnp.where(hit, local[None, :] + 1, 0), axis=1) - 1
    pick = (place[:, None] == jnp.arange(row_count, dtype=jnp.int32)[None, :]).astype(jnp.bfloat16)
    share = lax.dynamic_slice_in_dim(vectors, col * depth, depth, 0)
    take = lambda x: nt(pick, x, None).astype(jnp.bfloat16)
    sending = jnp.concatenate([take(share), take(integrals[0]), take(integrals[1])], axis=1)
    gathered = gather_slots(sending, owners, parts)
    gathered, left[0], right[1] = lax.optimization_barrier((gathered, left[0], right[1]))
    far = (hop(left[0], 1), hop(right[1], -1))
    gt, l0, l1, ft = factor(gathered, slot_of[:, None])
    shards = [x[p] for p in range(PANELS) for x in (right, far, left)]
    return apply_factors(vectors, integrals, shards, gt, l0, l1, ft)


def solution(mesh):
    torus = Mesh(
        mesh.devices.reshape(8, 4, 2, mesh.shape["cols"]), ("rows_0", "rows_1", "rows_2", "cols")
    )
    return jax.shard_map(
        per_device,
        mesh=torus,
        in_specs=(P(None, ROWS), P(None, "cols", ROWS), P()),
        out_specs=P(None, "cols", ROWS),
        check_vma=False,
    )
```

```python
import functools

import jax
import jax.numpy as jnp
from jax import lax
from jax.experimental import pallas as pl
from jax.experimental.pallas import tpu as pltpu
from jax.sharding import Mesh
from jax.sharding import PartitionSpec as P

PW = 256
PANELS = 2
SLOTS = 8
ROWS = ("rows_0", "rows_1", "rows_2")
HI = lax.Precision.HIGHEST
MESH = pl.DeviceIdType.MESH


def bsub(x, k):
    return jnp.broadcast_to(x[k:k+1, :], (8, 128))

def blane(x, k):
    return jnp.broadcast_to(x[:, k:k+1], (8, 128))

def factor_inverse_128(rows):
    sub = lax.broadcasted_iota(jnp.int32, (8, 128), 0)
    lane = lax.broadcasted_iota(jnp.int32, (8, 128), 1)
    out = []
    for s in range(16):
        base = 8 * s
        r = rows[s]
        cols = [blane(r, base + k) for k in range(8)]
        a = {}
        for k in range(8):
            for i in range(k, 8):
                a[i, k] = bsub(cols[k], i)
        unit, pivot = [], []
        for k in range(8):
            g = lambda i, j: a[max(i, j), min(i, j)]
            d = a[k, k]
            pivot.append(d)
            unit.append([g(k, j) for j in range(k)])
            p = 1.0 / d
            others = [i for i in range(8) if i != k]
            b = {i: g(i, k) * p for i in others}
            new = dict(a)
            for x, i in enumerate(others):
                for j in others[:x + 1]:
                    new[i, j] = a[i, j] - b[i] * g(j, k)
                new[max(i, k), min(i, k)] = b[i]
            new[k, k] = -p
            a = new
        def column(vals):
            v = vals[0]
            for i in range(1, 8):
                v = jnp.where(sub == i, vals[i], v)
            return v
        g = lambda i, j: a[max(i, j), min(i, j)]
        ninv = [column([g(i, k) for i in range(8)]) for k in range(8)]
        scale = lax.rsqrt(column(pivot))
        kcol = []
        for j in range(8):
            v = jnp.where(sub == j, scale, 0.0)
            for i in range(j + 1, 8):
                v = jnp.where(sub == i, -unit[i][j] * scale, v)
            kcol.append(v)
        inblock = (lane >= base) & (lane < base + 8)
        rp = jnp.where(inblock, jnp.where(lane - base == sub, 1.0, 0.0), r)
        brow = [bsub(rp, k) for k in range(8)]
        fin = kcol[0] * brow[0]
        for k in range(1, 8):
            fin = fin + kcol[k] * brow[k]
        out.append(jnp.where(lane < base + 8, fin, 0.0))
        if s == 15:
            break
        ny = ninv[0] * brow[0]
        for k in range(1, 8):
            ny = ny + ninv[k] * brow[k]
        yb = [bsub(ny, k) for k in range(8)]
        for t in range(s + 1, 16):
            rt = rows[t]
            c = [blane(rt, base + k) for k in range(8)]
            acc0 = c[0] * yb[0]
            acc1 = c[1] * yb[1]
            for k in range(2, 8, 2):
                acc0 = acc0 + c[k] * yb[k]
                acc1 = acc1 + c[k + 1] * yb[k + 1]
            rows[t] = jnp.where(inblock, 0.0, rt) + (acc0 + acc1)
    return out

def nt(a, b, precision=HI):
    return lax.dot_general(a, b, (((1,), (1,)), ((), ())), precision=precision, preferred_element_type=jnp.float32)

def nn(a, b, precision=HI):
    return lax.dot_general(a, b, (((1,), (0,)), ((), ())), precision=precision, preferred_element_type=jnp.float32)

def inverse_factor(a_ref, l_ref):
    half = lambda ref, r, c: ref[pl.ds(128 * r, 128), pl.ds(128 * c, 128)]
    w = factor_inverse_128([a_ref[pl.ds(8 * i, 8), pl.ds(0, 128)] for i in range(16)])
    for i in range(16):
        l_ref[pl.ds(8 * i, 8), pl.ds(0, 128)] = w[i]
    l11 = half(l_ref, 0, 0)
    t21 = nt(half(a_ref, 1, 0), l11)
    a_ref[pl.ds(128, 128), pl.ds(128, 128)] = half(a_ref, 1, 1) - nt(t21, t21)
    w = factor_inverse_128([a_ref[pl.ds(128 + 8 * i, 8), pl.ds(128, 128)] for i in range(16)])
    for i in range(16):
        l_ref[pl.ds(128 + 8 * i, 8), pl.ds(128, 128)] = w[i]
    l22 = half(l_ref, 1, 1)
    l_ref[pl.ds(128, 128), pl.ds(0, 128)] = -nn(l22, nn(t21, l11))
    l_ref[pl.ds(0, 128), pl.ds(128, 128)] = jnp.zeros((128, 128), jnp.float32)


def one_pass_nt(a, b):
    return nt(a, b, None)


def split(x):
    high = x.astype(jnp.bfloat16)
    return high, (x - high.astype(jnp.float32)).astype(jnp.bfloat16)


def place_pivots(pivot_ref, me, row_count):
    columns, places = [], None
    mine = me * PANELS * SLOTS + lax.broadcasted_iota(jnp.int32, (PANELS * SLOTS, PW), 0)
    for panel in range(PANELS):
        row = jnp.broadcast_to(pivot_ref[pl.ds(panel, 1), :], (PW, PW))
        col = row.T
        owner_row, owner_col = row // row_count, col // row_count
        same = owner_row == owner_col
        i = lax.broadcasted_iota(jnp.int32, (PW, PW), 0)
        j = lax.broadcasted_iota(jnp.int32, (PW, PW), 1)
        one = lambda mask: jnp.where(mask, 1, 0)
        rank_col = jnp.sum(one(same & (j < i)), axis=1, keepdims=True)
        rank_row = jnp.sum(one(same & (i < j)), axis=0, keepdims=True)
        columns.append((owner_col[:, :1] * PANELS + panel) * SLOTS + rank_col)
        slot_row = (owner_row[:1] * PANELS + panel) * SLOTS + rank_row
        local = row[:1] - me * row_count + 1
        found = jnp.sum(jnp.where(slot_row == mine, local, 0), axis=1, keepdims=True)
        places = found if places is None else places + found
    return jnp.concatenate(columns, axis=0), places - 1


def front_kernel(pivot_ref, v_ref, int_ref, gt_ref, l0_ref, l1_ref, ft_ref, shard_ref,
                 vy_ref, own_int_ref, own_ref, g_ref, i0_ref, i1_ref, a_ref, l_ref,
                 send_sem, recv_sem, local_sem):
    parts, deep, wide, lines, cols = g_ref.shape
    half = lines // 2
    z, x, c, y = (lax.axis_index(axis) for axis in (*ROWS, "cols"))
    handler = y // 2
    started = []
    depth = vy_ref.shape[0]
    width = int_ref.shape[1]
    row_count = v_ref.shape[1]

    barrier = pltpu.get_barrier_semaphore()
    greeted = 0
    for dz in range(deep):
        for other in range(2 * parts):
            if dz == 0 and other == 0:
                continue
            where = lax.rem(2 * y + c + other, 2 * parts)
            pl.semaphore_signal(
                barrier,
                device_id={"rows_0": lax.rem(z + dz, deep), "cols": where // 2, "rows_2": lax.rem(where, 2)},
                device_id_type=MESH,
            )
            greeted += 1
    for other in range(1, wide):
        pl.semaphore_signal(barrier, device_id={"rows_1": lax.rem(x + other, wide)}, device_id_type=MESH)
        greeted += 1

    loads = [
        pltpu.make_async_copy(v_ref.at[pl.ds(pl.multiple_of(y * depth, depth), depth)], vy_ref, local_sem.at[0]),
        pltpu.make_async_copy(int_ref, own_int_ref, local_sem.at[1]),
    ]
    for copy in loads:
        copy.start()

    me = (z * wide + x) * 2 + c
    slot_col, place = place_pivots(pivot_ref, me, row_count)
    pick = (lax.broadcasted_iota(jnp.int32, (half, row_count), 1) == place).astype(jnp.bfloat16)
    for copy in loads:
        copy.wait()
    own_ref[:, pl.ds(0, depth)] = one_pass_nt(pick, vy_ref[...]).astype(jnp.bfloat16)
    both = own_int_ref[...].reshape(PANELS * width, row_count)
    own_ref[:, pl.ds(depth, PANELS * width)] = one_pass_nt(pick, both).astype(jnp.bfloat16)
    pl.semaphore_wait(barrier, greeted)

    slot = [deep * parts]

    def send(part, to):
        i = slot[0]
        slot[0] += 1
        copy = pltpu.make_async_remote_copy(
            src_ref=part, dst_ref=part, send_sem=send_sem.at[i], recv_sem=recv_sem.at[i], device_id=to, device_id_type=MESH
        )
        copy.start()
        started.append(copy)
        return copy

    mine = g_ref.at[y, z, x, pl.ds(half * c, half)]
    here = handler == c
    away = jnp.logical_not(here)
    local = pltpu.make_async_copy(own_ref, mine, local_sem.at[2])

    def own_copy(dz, dy):
        return pltpu.make_async_remote_copy(
            src_ref=own_ref,
            dst_ref=mine,
            send_sem=send_sem.at[dz * parts + dy],
            recv_sem=recv_sem.at[dz * 4 + lax.rem(y, 2) * 2 + c],
            device_id={"rows_0": lax.rem(z + dz, deep), "cols": lax.rem(y + dy, parts), "rows_2": handler},
            device_id_type=MESH,
        )

    pl.when(here)(lambda: local.start())
    hops = [0] + [h for k in range(1, deep // 2) for h in (k, deep - k)] + [deep // 2]
    for dz in hops:
        for dy in range(parts):
            if dz == 0 and dy == 0:
                pl.when(away)(lambda: own_copy(0, 0).start())
            else:
                own_copy(dz, dy).start()
    pl.when(here)(lambda: local.wait())

    sibling = {"rows_2": 1 - c}
    pair = pl.ds(pl.multiple_of(2 * c, 2), 2)
    across = {k: [] for k in range(1, wide)}
    for dz in hops:
        at_z = lax.rem(z - dz + deep, deep)
        for p in range(2):
            for k in range(2):
                block = g_ref.at[2 * c + p, at_z, x, pl.ds(half * k, half)]
                copy = pltpu.make_async_remote_copy(
                    src_ref=block, dst_ref=block, send_sem=send_sem.at[0], recv_sem=recv_sem.at[dz * 4 + 2 * p + k],
                    device_id=sibling, device_id_type=MESH,
                )
                if dz == 0:
                    pl.when(jnp.logical_or(2 * c + p != y, c != k))(lambda copy=copy: copy.wait_recv())
                else:
                    copy.wait_recv()
        for dx in (1, wide - 1, 2):
            across[dx].append(send(g_ref.at[pair, at_z, x], {"rows_1": lax.rem(x + dx, wide)}))

    shards = []
    for k in range(1, parts):
        i = slot[0]
        slot[0] += 1
        copy = pltpu.make_async_remote_copy(
            src_ref=int_ref, dst_ref=shard_ref.at[k - 1], send_sem=send_sem.at[i], recv_sem=recv_sem.at[i],
            device_id={"cols": lax.rem(y - k + parts, parts)}, device_id_type=MESH,
        )
        copy.start()
        shards.append(copy)

    swapped = [send(g_ref.at[pair, :, x], sibling)]
    for dx in (1, wide - 1, 2):
        for copy in across[dx]:
            copy.wait_recv()
        swapped.append(send(g_ref.at[pair, :, lax.rem(x - dx + wide, wide)], sibling))
    for copy in swapped:
        copy.wait_recv()

    factor_panels(slot_col, g_ref, gt_ref, l0_ref, l1_ref, ft_ref, i0_ref, i1_ref, a_ref, l_ref)

    for copy in started:
        copy.wait_send()
    for dz in hops:
        for dy in range(parts):
            if dz == 0 and dy == 0:
                pl.when(away)(lambda: own_copy(0, 0).wait_send())
            else:
                own_copy(dz, dy).wait_send()
    for copy in shards:
        copy.wait()


def factor_panels(slot_col, g_ref, gt_ref, l0_ref, l1_ref, ft_ref, i0_ref, i1_ref, a_ref, l_ref):
    parts, deep, wide, lines, cols = g_ref.shape
    rows = deep * wide * lines
    pick = (lax.broadcasted_iota(jnp.int32, (2 * PW, rows), 1) == slot_col).astype(jnp.bfloat16)
    depth = gt_ref.shape[1] // parts
    width = PW // parts
    for y in range(parts):
        t = nn(pick, g_ref[y].reshape(rows, cols), None)
        gt_ref[:, pl.ds(depth * y, depth)] = t[:, :depth].astype(jnp.bfloat16)
        i0_ref[:, pl.ds(width * y, width)] = t[:, depth : depth + width]
        i1_ref[:, pl.ds(width * y, width)] = t[PW:, depth + width :]
    g0, g1 = gt_ref[pl.ds(0, PW), :], gt_ref[pl.ds(PW, PW), :]
    own = i0_ref[pl.ds(0, PW), :]
    a_ref[...] = 0.5 * (own + own.T) - one_pass_nt(g0, g0)
    inverse_factor(a_ref, l_ref)
    l0 = l_ref[...]
    high, low = split(l0)
    l0_ref[pl.ds(0, PW), :] = high
    l0_ref[pl.ds(PW, PW), :] = low
    later = i0_ref[pl.ds(PW, PW), :] - one_pass_nt(g1, g0)
    ft = nt(later, l0).astype(jnp.bfloat16)
    ft_ref[...] = ft
    own = i1_ref[...]
    a_ref[...] = 0.5 * (own + own.T) - one_pass_nt(g1, g1) - one_pass_nt(ft, ft)
    inverse_factor(a_ref, l_ref)
    high, low = split(l_ref[...])
    l1_ref[pl.ds(0, PW), :] = high
    l1_ref[pl.ds(PW, PW), :] = low


def front(pivots, vectors, integrals):
    panels, width, columns = integrals.shape
    deep, wide, parts = lax.axis_size(ROWS[0]), lax.axis_size(ROWS[1]), lax.axis_size("cols")
    depth = vectors.shape[0]
    lines = PANELS * SLOTS
    share = depth // parts
    across = share + panels * width
    full = jax.ShapeDtypeStruct
    bf, f32 = jnp.bfloat16, jnp.float32
    vmem, hbm = pl.BlockSpec(memory_space=pltpu.VMEM), pl.BlockSpec(memory_space=pl.ANY)
    copies = deep * parts + deep * (wide - 1) + wide + parts - 1
    return pl.pallas_call(
        front_kernel,
        in_specs=[vmem, hbm, hbm],
        out_specs=[vmem, vmem, vmem, vmem, hbm],
        out_shape=(
            full((2 * PW, depth), bf),
            full((2 * PW, PW), bf),
            full((2 * PW, PW), bf),
            full((PW, PW), bf),
            full((parts - 1, *integrals.shape), bf),
        ),
        scratch_shapes=[
            pltpu.VMEM((share, columns), bf),
            pltpu.VMEM(integrals.shape, bf),
            pltpu.VMEM((lines, across), bf),
            pltpu.VMEM((parts, deep, wide, 2 * lines, across), bf),
            pltpu.VMEM((2 * PW, PW), f32),
            pltpu.VMEM((PW, PW), f32),
            pltpu.VMEM((PW, PW), f32),
            pltpu.VMEM((PW, PW), f32),
            pltpu.SemaphoreType.DMA((copies,)),
            pltpu.SemaphoreType.DMA((copies,)),
            pltpu.SemaphoreType.DMA((3,)),
        ],
        compiler_params=pltpu.CompilerParams(collective_id=0, has_side_effects=True, vmem_limit_bytes=56 << 20),
        cost_estimate=pl.CostEstimate(flops=2 * 10**9, bytes_accessed=40 << 20, transcendentals=0),
        name="front",
    )(pivots, vectors, integrals)


def apply_kernel(v_ref, own_ref, shard_ref, gt_ref, l0_ref, l1_ref, ft_ref, out_ref, r_ref):
    me = lax.axis_index("cols")
    width = own_ref.shape[1]

    def residual(panel):
        r_ref[...] = -nn(gt_ref[pl.ds(PW * panel, PW), :], v_ref[...], None)
        for k in range(4):
            at = pl.ds(pl.multiple_of(lax.rem(me + k, 4) * width, width), width)
            shard = own_ref[panel] if k == 0 else shard_ref[k - 1, panel]
            r_ref[at, :] += shard.astype(jnp.float32)

    mine = pl.multiple_of(me * width, width)
    residual(0)
    high, low = split(r_ref[...])
    both = nn(l0_ref[...], high, None)
    x = both[:PW] + both[PW:] + nn(l0_ref[pl.ds(0, PW), :], low, None)
    rounded = x.astype(jnp.bfloat16)
    r_ref[...] = x
    out_ref[0] = r_ref[pl.ds(mine, width), :]
    residual(1)
    r = r_ref[...] - lax.dot_general(ft_ref[...], rounded, (((1,), (0,)), ((), ())), preferred_element_type=jnp.float32)
    high, low = split(r)
    lh = l1_ref[pl.ds(mine, width), :]
    ll = l1_ref[pl.ds(pl.multiple_of(PW + mine, width), width), :]
    out_ref[1] = nn(lh, high, None) + (nn(ll, high, None) + nn(lh, low, None))


def apply_factors(vectors, integrals, shards, gt, l0, l1, ft):
    depth, columns = vectors.shape
    width = integrals.shape[1]
    chunk = 512
    whole = lambda x: pl.BlockSpec(x.shape, lambda j: (0,) * x.ndim, pipeline_mode=pl.Buffered(1))
    part = pl.BlockSpec((PANELS, width, chunk), lambda j: (0, 0, j))
    others = pl.BlockSpec((shards.shape[0], PANELS, width, chunk), lambda j: (0, 0, 0, j))
    return pl.pallas_call(
        apply_kernel,
        grid=(columns // chunk,),
        in_specs=[pl.BlockSpec((depth, chunk), lambda j: (0, j)), part, others] + [whole(x) for x in (gt, l0, l1, ft)],
        out_specs=part,
        out_shape=jax.ShapeDtypeStruct((PANELS, width, columns), jnp.float32),
        scratch_shapes=[pltpu.VMEM((PW, chunk), jnp.float32)],
        compiler_params=pltpu.CompilerParams(vmem_limit_bytes=60 << 20),
        cost_estimate=pl.CostEstimate(flops=7 * 10**9, bytes_accessed=16 << 20, transcendentals=0),
        name="apply",
    )(vectors, integrals, shards, gt, l0, l1, ft)


def per_device(vectors, integrals, pivots):
    gt, l0, l1, ft, shards = front(pivots, vectors, integrals)
    return apply_factors(vectors, integrals, shards, gt, l0, l1, ft)


def solution(mesh):
    torus = Mesh(
        mesh.devices.reshape(8, 4, 2, mesh.shape["cols"]), ("rows_0", "rows_1", "rows_2", "cols")
    )
    return jax.shard_map(
        per_device,
        mesh=torus,
        in_specs=(P(None, ROWS), P(None, "cols", ROWS), P()),
        out_specs=P(None, "cols", ROWS),
        check_vma=False,
    )
```

```python
import functools

import jax
import jax.numpy as jnp
from jax import lax
from jax.experimental import pallas as pl
from jax.experimental.pallas import tpu as pltpu
from jax.sharding import Mesh
from jax.sharding import PartitionSpec as P

PW = 256
PANELS = 2
SLOTS = 8
ROWS = ("rows_0", "rows_1", "rows_2")
HI = lax.Precision.HIGHEST
MESH = pl.DeviceIdType.MESH


def bsub(x, k):
    return jnp.broadcast_to(x[k:k+1, :], (8, 128))

def blane(x, k):
    return jnp.broadcast_to(x[:, k:k+1], (8, 128))

def factor_inverse_128(rows, meanwhile):
    sub = lax.broadcasted_iota(jnp.int32, (8, 128), 0)
    lane = lax.broadcasted_iota(jnp.int32, (8, 128), 1)
    out = []
    for s in range(16):
        meanwhile(s)
        base = 8 * s
        r = rows[s]
        cols = [blane(r, base + k) for k in range(8)]
        a = {}
        for k in range(8):
            for i in range(k, 8):
                a[i, k] = bsub(cols[k], i)
        unit, pivot = [], []
        for k in range(8):
            g = lambda i, j: a[max(i, j), min(i, j)]
            d = a[k, k]
            pivot.append(d)
            unit.append([g(k, j) for j in range(k)])
            p = 1.0 / d
            others = [i for i in range(8) if i != k]
            b = {i: g(i, k) * p for i in others}
            new = dict(a)
            for x, i in enumerate(others):
                for j in others[:x + 1]:
                    new[i, j] = a[i, j] - b[i] * g(j, k)
                new[max(i, k), min(i, k)] = b[i]
            new[k, k] = -p
            a = new
        def column(vals):
            v = vals[0]
            for i in range(1, 8):
                v = jnp.where(sub == i, vals[i], v)
            return v
        g = lambda i, j: a[max(i, j), min(i, j)]
        ninv = [column([g(i, k) for i in range(8)]) for k in range(8)]
        scale = lax.rsqrt(column(pivot))
        kcol = []
        for j in range(8):
            v = jnp.where(sub == j, scale, 0.0)
            for i in range(j + 1, 8):
                v = jnp.where(sub == i, -unit[i][j] * scale, v)
            kcol.append(v)
        inblock = (lane >= base) & (lane < base + 8)
        rp = jnp.where(inblock, jnp.where(lane - base == sub, 1.0, 0.0), r)
        brow = [bsub(rp, k) for k in range(8)]
        fin = kcol[0] * brow[0]
        for k in range(1, 8):
            fin = fin + kcol[k] * brow[k]
        out.append(jnp.where(lane < base + 8, fin, 0.0))
        if s == 15:
            break
        ny = ninv[0] * brow[0]
        for k in range(1, 8):
            ny = ny + ninv[k] * brow[k]
        yb = [bsub(ny, k) for k in range(8)]
        for t in range(s + 1, 16):
            rt = rows[t]
            c = [blane(rt, base + k) for k in range(8)]
            acc0 = c[0] * yb[0]
            acc1 = c[1] * yb[1]
            for k in range(2, 8, 2):
                acc0 = acc0 + c[k] * yb[k]
                acc1 = acc1 + c[k + 1] * yb[k + 1]
            rows[t] = jnp.where(inblock, 0.0, rt) + (acc0 + acc1)
    return out

def nt(a, b, precision=HI):
    return lax.dot_general(a, b, (((1,), (1,)), ((), ())), precision=precision, preferred_element_type=jnp.float32)

def nn(a, b, precision=HI):
    return lax.dot_general(a, b, (((1,), (0,)), ((), ())), precision=precision, preferred_element_type=jnp.float32)

def inverse_factor(a_ref, l_ref, meanwhile):
    half = lambda ref, r, c: ref[pl.ds(128 * r, 128), pl.ds(128 * c, 128)]
    w = factor_inverse_128([a_ref[pl.ds(8 * i, 8), pl.ds(0, 128)] for i in range(16)], lambda s: meanwhile(s))
    for i in range(16):
        l_ref[pl.ds(8 * i, 8), pl.ds(0, 128)] = w[i]
    l11 = half(l_ref, 0, 0)
    t21 = nt(half(a_ref, 1, 0), l11)
    a_ref[pl.ds(128, 128), pl.ds(128, 128)] = half(a_ref, 1, 1) - nt(t21, t21)
    w = factor_inverse_128([a_ref[pl.ds(128 + 8 * i, 8), pl.ds(128, 128)] for i in range(16)], lambda s: meanwhile(16 + s))
    for i in range(16):
        l_ref[pl.ds(128 + 8 * i, 8), pl.ds(128, 128)] = w[i]
    l22 = half(l_ref, 1, 1)
    l_ref[pl.ds(128, 128), pl.ds(0, 128)] = -nn(l22, nn(t21, l11))
    l_ref[pl.ds(0, 128), pl.ds(128, 128)] = jnp.zeros((128, 128), jnp.float32)


def one_pass_nt(a, b):
    return nt(a, b, None)


def split(x):
    high = x.astype(jnp.bfloat16)
    return high, (x - high.astype(jnp.float32)).astype(jnp.bfloat16)


def place_pivots(pivot_ref, me, row_count):
    columns, places = [], None
    mine = me * PANELS * SLOTS + lax.broadcasted_iota(jnp.int32, (PANELS * SLOTS, PW), 0)
    for panel in range(PANELS):
        row = jnp.broadcast_to(pivot_ref[pl.ds(panel, 1), :], (PW, PW))
        col = row.T
        owner_row, owner_col = row // row_count, col // row_count
        same = owner_row == owner_col
        i = lax.broadcasted_iota(jnp.int32, (PW, PW), 0)
        j = lax.broadcasted_iota(jnp.int32, (PW, PW), 1)
        one = lambda mask: jnp.where(mask, 1, 0)
        rank_col = jnp.sum(one(same & (j < i)), axis=1, keepdims=True)
        rank_row = jnp.sum(one(same & (i < j)), axis=0, keepdims=True)
        columns.append((owner_col[:, :1] * PANELS + panel) * SLOTS + rank_col)
        slot_row = (owner_row[:1] * PANELS + panel) * SLOTS + rank_row
        local = row[:1] - me * row_count + 1
        found = jnp.sum(jnp.where(slot_row == mine, local, 0), axis=1, keepdims=True)
        places = found if places is None else places + found
    return jnp.concatenate(columns, axis=0), places - 1


def front_kernel(pivot_ref, v_ref, int_ref, l0_ref, l1_ref, ft_ref, shard_ref, p_ref,
                 gt_ref, all_v_ref, prod_ref, own_int_ref, own_ref, g_ref, i0_ref, i1_ref, a_ref, l_ref,
                 send_sem, recv_sem, local_sem):
    parts, deep, wide, lines, cols = g_ref.shape
    half = lines // 2
    z, x, c, y = (lax.axis_index(axis) for axis in (*ROWS, "cols"))
    handler = y // 2
    started = []
    depth = v_ref.shape[0] // parts
    width = int_ref.shape[1]
    row_count = v_ref.shape[1]

    barrier = pltpu.get_barrier_semaphore()

    def greet(**to):
        pl.semaphore_signal(barrier, device_id=to, device_id_type=MESH)

    for dz in range(deep):
        for p in range(2):
            for k in range(2):
                greet(rows_0=lax.rem(z + dz, deep), cols=2 * c + p, rows_2=k)
    for other in range(1, wide):
        greet(rows_1=lax.rem(x + other, wide))
    greet(cols=lax.rem(y + 1, parts))
    greet(cols=lax.rem(y + parts - 1, parts))
    greet(rows_2=1 - c)
    greeted = 4 * deep + wide + 2

    loads = [pltpu.make_async_copy(int_ref, own_int_ref, local_sem.at[0])]
    for k in range(parts):
        share = pl.ds(pl.multiple_of(lax.rem(y + k, parts) * depth, depth), depth)
        loads.append(pltpu.make_async_copy(v_ref.at[share], all_v_ref.at[share], local_sem.at[1 + k]))
    for copy in loads:
        copy.start()

    me = (z * wide + x) * 2 + c
    slot_col, place = place_pivots(pivot_ref, me, row_count)
    pick = (lax.broadcasted_iota(jnp.int32, (half, row_count), 1) == place).astype(jnp.bfloat16)
    for copy in loads[:2]:
        copy.wait()
    share = all_v_ref[pl.ds(pl.multiple_of(y * depth, depth), depth), :]
    own_ref[:, pl.ds(0, depth)] = one_pass_nt(pick, share).astype(jnp.bfloat16)
    both = own_int_ref[...].reshape(PANELS * width, row_count)
    own_ref[:, pl.ds(depth, PANELS * width)] = one_pass_nt(pick, both).astype(jnp.bfloat16)
    pl.semaphore_wait(barrier, greeted)

    slot = [deep * parts]

    def send(part, to):
        i = slot[0]
        slot[0] += 1
        copy = pltpu.make_async_remote_copy(
            src_ref=part, dst_ref=part, send_sem=send_sem.at[i], recv_sem=recv_sem.at[i], device_id=to, device_id_type=MESH
        )
        copy.start()
        started.append(copy)
        return copy

    mine = g_ref.at[y, z, x, pl.ds(half * c, half)]
    here = handler == c
    away = jnp.logical_not(here)
    local = pltpu.make_async_copy(own_ref, mine, local_sem.at[5])

    def own_copy(dz, dy):
        return pltpu.make_async_remote_copy(
            src_ref=own_ref,
            dst_ref=mine,
            send_sem=send_sem.at[dz * parts + dy],
            recv_sem=recv_sem.at[dz * 4 + lax.rem(y, 2) * 2 + c],
            device_id={"rows_0": lax.rem(z + dz, deep), "cols": lax.rem(y + dy, parts), "rows_2": handler},
            device_id_type=MESH,
        )

    pl.when(here)(lambda: local.start())
    hops = [0] + [h for k in range(1, deep // 2) for h in (k, deep - k)] + [deep // 2]
    for dz in hops:
        for dy in range(parts):
            if dz == 0 and dy == 0:
                pl.when(away)(lambda: own_copy(0, 0).start())
            else:
                own_copy(dz, dy).start()
    pl.when(here)(lambda: local.wait())

    sibling = {"rows_2": 1 - c}
    pair = pl.ds(pl.multiple_of(2 * c, 2), 2)
    across = {k: [] for k in range(1, wide)}
    for dz in hops:
        at_z = lax.rem(z - dz + deep, deep)
        for p in range(2):
            for k in range(2):
                block = g_ref.at[2 * c + p, at_z, x, pl.ds(half * k, half)]
                copy = pltpu.make_async_remote_copy(
                    src_ref=block, dst_ref=block, send_sem=send_sem.at[0], recv_sem=recv_sem.at[dz * 4 + 2 * p + k],
                    device_id=sibling, device_id_type=MESH,
                )
                if dz == 0:
                    pl.when(jnp.logical_or(2 * c + p != y, c != k))(lambda copy=copy: copy.wait_recv())
                else:
                    copy.wait_recv()
        for dx in (1, wide - 1, 2):
            across[dx].append(send(g_ref.at[pair, at_z, x], {"rows_1": lax.rem(x + dx, wide)}))

    def pass_on(src, dst, by):
        i = slot[0]
        slot[0] += 1
        copy = pltpu.make_async_remote_copy(
            src_ref=src, dst_ref=dst, send_sem=send_sem.at[i], recv_sem=recv_sem.at[i],
            device_id={"cols": lax.rem(y + by + parts, parts)}, device_id_type=MESH,
        )
        copy.start()
        started.append(copy)
        return copy

    to_left = pass_on(int_ref, shard_ref.at[0], -1)
    to_right = pass_on(int_ref, shard_ref.at[2], 1)

    swapped = [send(g_ref.at[pair, :, x], sibling)]
    for dx in (1, wide - 1, 2):
        for copy in across[dx]:
            copy.wait_recv()
        swapped.append(send(g_ref.at[pair, :, lax.rem(x - dx + wide, wide)], sibling))
    for copy in swapped:
        copy.wait_recv()

    onward = []

    def relay():
        to_left.wait_recv()
        to_right.wait_recv()
        onward.append(pass_on(shard_ref.at[2, 0], shard_ref.at[1, 0], 1))
        onward.append(pass_on(shard_ref.at[0, 1], shard_ref.at[1, 1], -1))

    for copy in loads[2:]:
        copy.wait()
    written = []

    def multiply(panel, step):
        if step % 2 == 0:
            at = pl.ds(PW * (step // 2), PW)
            prod_ref[panel, :, at] = nn(gt_ref[pl.ds(PW * panel, PW), :], all_v_ref[:, at], None)

    def write(panel):
        copy = pltpu.make_async_copy(prod_ref.at[panel], p_ref.at[panel], local_sem.at[6 + panel])
        copy.start()
        written.append(copy)

    factor_panels(
        slot_col, g_ref, gt_ref, l0_ref, l1_ref, ft_ref, i0_ref, i1_ref, a_ref, l_ref, multiply, (write, relay)
    )
    for copy in written:
        copy.wait()
    for copy in onward:
        copy.wait_recv()

    for copy in started:
        copy.wait_send()
    for dz in hops:
        for dy in range(parts):
            if dz == 0 and dy == 0:
                pl.when(away)(lambda: own_copy(0, 0).wait_send())
            else:
                own_copy(dz, dy).wait_send()


def factor_panels(slot_col, g_ref, gt_ref, l0_ref, l1_ref, ft_ref, i0_ref, i1_ref, a_ref, l_ref, multiply, between):
    write, relay = between
    parts, deep, wide, lines, cols = g_ref.shape
    rows = deep * wide * lines
    pick = (lax.broadcasted_iota(jnp.int32, (2 * PW, rows), 1) == slot_col).astype(jnp.bfloat16)
    depth = gt_ref.shape[1] // parts
    width = PW // parts
    for y in range(parts):
        t = nn(pick, g_ref[y].reshape(rows, cols), None)
        gt_ref[:, pl.ds(depth * y, depth)] = t[:, :depth].astype(jnp.bfloat16)
        i0_ref[:, pl.ds(width * y, width)] = t[:, depth : depth + width]
        i1_ref[:, pl.ds(width * y, width)] = t[PW:, depth + width :]
    g0, g1 = gt_ref[pl.ds(0, PW), :], gt_ref[pl.ds(PW, PW), :]
    own = i0_ref[pl.ds(0, PW), :]
    a_ref[...] = 0.5 * (own + own.T) - one_pass_nt(g0, g0)
    inverse_factor(a_ref, l_ref, lambda step: multiply(0, step))
    write(0)
    relay()
    l0 = l_ref[...]
    high, low = split(l0)
    l0_ref[pl.ds(0, PW), :] = high
    l0_ref[pl.ds(PW, PW), :] = low
    later = i0_ref[pl.ds(PW, PW), :] - one_pass_nt(g1, g0)
    ft = nt(later, l0).astype(jnp.bfloat16)
    ft_ref[...] = ft
    own = i1_ref[...]
    a_ref[...] = 0.5 * (own + own.T) - one_pass_nt(g1, g1) - one_pass_nt(ft, ft)
    inverse_factor(a_ref, l_ref, lambda step: multiply(1, step))
    write(1)
    high, low = split(l_ref[...])
    l1_ref[pl.ds(0, PW), :] = high
    l1_ref[pl.ds(PW, PW), :] = low


def front(pivots, vectors, integrals):
    panels, width, columns = integrals.shape
    deep, wide, parts = lax.axis_size(ROWS[0]), lax.axis_size(ROWS[1]), lax.axis_size("cols")
    depth = vectors.shape[0]
    lines = PANELS * SLOTS
    share = depth // parts
    across = share + panels * width
    full = jax.ShapeDtypeStruct
    bf, f32 = jnp.bfloat16, jnp.float32
    vmem, hbm = pl.BlockSpec(memory_space=pltpu.VMEM), pl.BlockSpec(memory_space=pl.ANY)
    copies = deep * parts + deep * (wide - 1) + wide + 4
    return pl.pallas_call(
        front_kernel,
        in_specs=[vmem, hbm, hbm],
        out_specs=[vmem, vmem, vmem, hbm, hbm],
        out_shape=(
            full((2 * PW, PW), bf),
            full((2 * PW, PW), bf),
            full((PW, PW), bf),
            full((parts - 1, *integrals.shape), bf),
            full((panels, PW, columns), f32),
        ),
        scratch_shapes=[
            pltpu.VMEM((2 * PW, depth), bf),
            pltpu.VMEM((depth, columns), bf),
            pltpu.VMEM((panels, PW, columns), f32),
            pltpu.VMEM(integrals.shape, bf),
            pltpu.VMEM((lines, across), bf),
            pltpu.VMEM((parts, deep, wide, 2 * lines, across), bf),
            pltpu.VMEM((2 * PW, PW), f32),
            pltpu.VMEM((PW, PW), f32),
            pltpu.VMEM((PW, PW), f32),
            pltpu.VMEM((PW, PW), f32),
            pltpu.SemaphoreType.DMA((copies,)),
            pltpu.SemaphoreType.DMA((copies,)),
            pltpu.SemaphoreType.DMA((8,)),
        ],
        compiler_params=pltpu.CompilerParams(collective_id=0, has_side_effects=True, vmem_limit_bytes=56 << 20),
        cost_estimate=pl.CostEstimate(flops=2 * 10**9, bytes_accessed=40 << 20, transcendentals=0),
        name="front",
    )(pivots, vectors, integrals)


def apply_kernel(p_ref, own_ref, shard_ref, l0_ref, l1_ref, ft_ref, out_ref, r_ref, x_ref):
    me = lax.axis_index("cols")
    width = own_ref.shape[1]
    parts = shard_ref.shape[0] + 1
    for panel in range(PANELS):
        for k in range(parts):
            at = pl.ds(pl.multiple_of(lax.rem(me + k, parts) * width, width), width)
            shard = own_ref[panel] if k == 0 else shard_ref[k - 1, panel]
            r_ref[panel, at, :] = shard.astype(jnp.float32) - p_ref[panel, at, :]
    mine = pl.multiple_of(me * width, width)
    high, low = split(r_ref[0])
    both = nn(l0_ref[...], high, None)
    x = both[:PW] + both[PW:] + nn(l0_ref[pl.ds(0, PW), :], low, None)
    x_ref[...] = x
    out_ref[0] = x_ref[pl.ds(mine, width), :]
    turned = lax.dot_general(
        ft_ref[...], x.astype(jnp.bfloat16), (((1,), (0,)), ((), ())), preferred_element_type=jnp.float32
    )
    high, low = split(r_ref[1] - turned)
    lh = l1_ref[pl.ds(mine, width), :]
    ll = l1_ref[pl.ds(pl.multiple_of(PW + mine, width), width), :]
    out_ref[1] = nn(lh, high, None) + (nn(ll, high, None) + nn(lh, low, None))


def apply_factors(products, integrals, shards, l0, l1, ft):
    panels, width, columns = integrals.shape
    chunk = 1024
    whole = lambda x: pl.BlockSpec(x.shape, lambda j: (0,) * x.ndim, pipeline_mode=pl.Buffered(1))
    part = lambda *lead: pl.BlockSpec((*lead, chunk), lambda j: (0,) * len(lead) + (j,))
    return pl.pallas_call(
        apply_kernel,
        grid=(columns // chunk,),
        in_specs=[part(panels, PW), part(panels, width), part(shards.shape[0], panels, width)] + [whole(x) for x in (l0, l1, ft)],
        out_specs=part(panels, width),
        out_shape=jax.ShapeDtypeStruct((panels, width, columns), jnp.float32),
        scratch_shapes=[pltpu.VMEM((panels, PW, chunk), jnp.float32), pltpu.VMEM((PW, chunk), jnp.float32)],
        compiler_params=pltpu.CompilerParams(vmem_limit_bytes=60 << 20),
        cost_estimate=pl.CostEstimate(flops=3 * 10**9, bytes_accessed=16 << 20, transcendentals=0),
        name="apply",
    )(products, integrals, shards, l0, l1, ft)


def per_device(vectors, integrals, pivots):
    l0, l1, ft, shards, products = front(pivots, vectors, integrals)
    return apply_factors(products, integrals, shards, l0, l1, ft)


def solution(mesh):
    torus = Mesh(
        mesh.devices.reshape(8, 4, 2, mesh.shape["cols"]), ("rows_0", "rows_1", "rows_2", "cols")
    )
    return jax.shard_map(
        per_device,
        mesh=torus,
        in_specs=(P(None, ROWS), P(None, "cols", ROWS), P()),
        out_specs=P(None, "cols", ROWS),
        check_vma=False,
    )
```

```python
import functools

import jax
import jax.numpy as jnp
from jax import lax
from jax.experimental import pallas as pl
from jax.experimental.pallas import tpu as pltpu
from jax.sharding import Mesh
from jax.sharding import PartitionSpec as P

PW = 256
PANELS = 2
SLOTS = 8
ROWS = ("rows_0", "rows_1", "rows_2")
HI = lax.Precision.HIGHEST
MESH = pl.DeviceIdType.MESH


def total(terms):
    while len(terms) > 1:
        terms = [a + b for a, b in zip(terms[::2], terms[1::2])] + terms[len(terms) & ~1 :]
    return terms[0]


def bsub(x, k):
    return jnp.broadcast_to(x[k:k+1, :], (8, 128))

def blane(x, k):
    return jnp.broadcast_to(x[:, k:k+1], (8, 128))

def factor_inverse_128(rows, tmp_ref, meanwhile):
    sub = lax.broadcasted_iota(jnp.int32, (8, 128), 0)
    lane = lax.broadcasted_iota(jnp.int32, (8, 128), 1)
    out = []
    for s in range(16):
        meanwhile(s)
        base = 8 * s
        r = rows[s]
        cols = [blane(r, base + k) for k in range(8)]
        a = {}
        for k in range(8):
            tmp_ref[s, k] = cols[k]
        for k in range(8):
            for i in range(k, 8):
                a[i, k] = tmp_ref[s, k, pl.ds(i, 8, stride=0), :]
        unit, pivot = [], []
        for k in range(0, 8, 2):
            g = lambda i, j: a[max(i, j), min(i, j)]
            n = k + 1
            e, f, h = a[k, k], a[n, k], a[n, n]
            p = 1.0 / (e * h - f * f)
            t = f / e
            unit.append([g(k, j) for j in range(k)])
            unit.append([g(n, j) - t * g(k, j) for j in range(k)] + [t])
            pivot += [e, h - f * t]
            m = (h * p, -f * p, e * p)
            others = [i for i in range(8) if i not in (k, n)]
            w = {i: (g(i, k) * m[0] + g(i, n) * m[1], g(i, k) * m[1] + g(i, n) * m[2]) for i in others}
            new = dict(a)
            for x, i in enumerate(others):
                for j in others[: x + 1]:
                    new[i, j] = a[i, j] - (w[i][0] * g(j, k) + w[i][1] * g(j, n))
                new[max(i, k), min(i, k)] = w[i][0]
                new[max(i, n), min(i, n)] = w[i][1]
            new[k, k], new[n, k], new[n, n] = -m[0], -m[1], -m[2]
            a = new
        def column(vals):
            bit = 1
            while len(vals) > 1:
                vals = [jnp.where((sub & bit) > 0, b, a) for a, b in zip(vals[::2], vals[1::2])]
                bit *= 2
            return vals[0]
        g = lambda i, j: a[max(i, j), min(i, j)]
        ninv = [column([g(i, k) for i in range(8)]) for k in range(8)]
        scale = lax.rsqrt(column(pivot))
        kcol = []
        for j in range(8):
            v = jnp.where(sub == j, scale, 0.0)
            for i in range(j + 1, 8):
                v = jnp.where(sub == i, -unit[i][j] * scale, v)
            kcol.append(v)
        inblock = (lane >= base) & (lane < base + 8)
        rp = jnp.where(inblock, jnp.where(lane - base == sub, 1.0, 0.0), r)
        tmp_ref[s, 8] = rp
        brow = [tmp_ref[s, 8, pl.ds(k, 8, stride=0), :] for k in range(8)]
        fin = total([kcol[k] * brow[k] for k in range(8)])
        out.append(jnp.where(lane < base + 8, fin, 0.0))
        if s == 15:
            break
        ny = total([ninv[k] * brow[k] for k in range(8)])
        tmp_ref[s, 9] = ny
        yb = [tmp_ref[s, 9, pl.ds(k, 8, stride=0), :] for k in range(8)]
        for t in range(s + 1, 16):
            rt = rows[t]
            c = [blane(rt, base + k) for k in range(8)]
            acc = total([c[k] * yb[k] for k in range(8)])
            rows[t] = jnp.where(inblock, 0.0, rt) + acc
    return out

def nt(a, b, precision=HI):
    return lax.dot_general(a, b, (((1,), (1,)), ((), ())), precision=precision, preferred_element_type=jnp.float32)

def nn(a, b, precision=HI):
    return lax.dot_general(a, b, (((1,), (0,)), ((), ())), precision=precision, preferred_element_type=jnp.float32)

def inverse_factor(a_ref, l_ref, tmp_ref, meanwhile):
    half = lambda ref, r, c: ref[pl.ds(128 * r, 128), pl.ds(128 * c, 128)]
    w = factor_inverse_128([a_ref[pl.ds(8 * i, 8), pl.ds(0, 128)] for i in range(16)], tmp_ref.at[0], meanwhile)
    for i in range(16):
        l_ref[pl.ds(8 * i, 8), pl.ds(0, 128)] = w[i]
    l11 = half(l_ref, 0, 0)
    t21 = nt(half(a_ref, 1, 0), l11)
    a_ref[pl.ds(128, 128), pl.ds(128, 128)] = half(a_ref, 1, 1) - nt(t21, t21)
    w = factor_inverse_128([a_ref[pl.ds(128 + 8 * i, 8), pl.ds(128, 128)] for i in range(16)], tmp_ref.at[1], lambda s: meanwhile(16 + s))
    for i in range(16):
        l_ref[pl.ds(128 + 8 * i, 8), pl.ds(128, 128)] = w[i]
    l22 = half(l_ref, 1, 1)
    l_ref[pl.ds(128, 128), pl.ds(0, 128)] = -nn(l22, nn(t21, l11))
    l_ref[pl.ds(0, 128), pl.ds(128, 128)] = jnp.zeros((128, 128), jnp.float32)


def one_pass_nt(a, b):
    return nt(a, b, None)


def split(x):
    high = x.astype(jnp.bfloat16)
    return high, (x - high.astype(jnp.float32)).astype(jnp.bfloat16)


def place_pivots(pivot_ref, me, row_count):
    columns, places = [], []
    mine = me * SLOTS + lax.broadcasted_iota(jnp.int32, (SLOTS, PW), 0)
    for panel in range(PANELS):
        row = jnp.broadcast_to(pivot_ref[pl.ds(panel, 1), :], (PW, PW))
        col = row.T
        owner_row, owner_col = row // row_count, col // row_count
        same = owner_row == owner_col
        i = lax.broadcasted_iota(jnp.int32, (PW, PW), 0)
        j = lax.broadcasted_iota(jnp.int32, (PW, PW), 1)
        one = lambda mask: jnp.where(mask, 1, 0)
        rank_col = jnp.sum(one(same & (j < i)), axis=1, keepdims=True)
        rank_row = jnp.sum(one(same & (i < j)), axis=0, keepdims=True)
        columns.append(owner_col[:, :1] * SLOTS + rank_col)
        slot_row = owner_row[:1] * SLOTS + rank_row
        local = row[:1] - me * row_count + 1
        places.append(jnp.sum(jnp.where(slot_row == mine, local, 0), axis=1, keepdims=True) - 1)
    return columns, jnp.concatenate(places, axis=0)


def front_kernel(pivot_ref, v_ref, int_ref, l0_ref, l1_ref, ft_ref, shard_ref, p_ref,
                 gt_ref, all_v_ref, prod_ref, own_int_ref, land_ref, own_ref, g_ref, i0_ref, i1_ref, a_ref, l_ref, tmp_ref,
                 send_sem, recv_sem, local_sem):
    parts, deep, wide = g_ref.shape[1:4]
    z, x, c, y = (lax.axis_index(axis) for axis in (*ROWS, "cols"))
    handler = y // 2
    started = []
    depth = v_ref.shape[0] // parts
    width = int_ref.shape[1]
    row_count = v_ref.shape[1]

    barrier = pltpu.get_barrier_semaphore()

    def greet(**to):
        pl.semaphore_signal(barrier, device_id=to, device_id_type=MESH)

    for dz in range(deep):
        for p in range(2):
            for k in range(2):
                greet(rows_0=lax.rem(z + dz, deep), cols=2 * c + p, rows_2=k)
    for other in range(1, wide):
        greet(rows_1=lax.rem(x + other, wide))
    greet(cols=lax.rem(y + 1, parts))
    greet(cols=lax.rem(y + parts - 1, parts))
    greet(rows_2=1 - c)
    greeted = 4 * deep + wide + 2

    loads = [pltpu.make_async_copy(int_ref, own_int_ref, local_sem.at[0])]
    for k in range(parts):
        share = pl.ds(pl.multiple_of(lax.rem(y + k, parts) * depth, depth), depth)
        loads.append(pltpu.make_async_copy(v_ref.at[share], all_v_ref.at[share], local_sem.at[1 + k]))
    for copy in loads:
        copy.start()

    me = (z * wide + x) * 2 + c
    slot_col, place = place_pivots(pivot_ref, me, row_count)
    pick = (lax.broadcasted_iota(jnp.int32, (PANELS * SLOTS, row_count), 1) == place).astype(jnp.bfloat16)
    for copy in loads[:2]:
        copy.wait()
    share = all_v_ref[pl.ds(pl.multiple_of(y * depth, depth), depth), :]
    taken = one_pass_nt(pick, share).astype(jnp.bfloat16)
    own_ref[:, :, pl.ds(0, depth)] = taken.reshape(PANELS, SLOTS, depth)
    both = own_int_ref[...].reshape(PANELS * width, row_count)
    taken = one_pass_nt(pick, both).astype(jnp.bfloat16)
    own_ref[:, :, pl.ds(depth, PANELS * width)] = taken.reshape(PANELS, SLOTS, PANELS * width)
    pl.semaphore_wait(barrier, greeted)

    slot = [deep * parts]

    def send(part, to):
        i = slot[0]
        slot[0] += 1
        copy = pltpu.make_async_remote_copy(
            src_ref=part, dst_ref=part, send_sem=send_sem.at[i], recv_sem=recv_sem.at[i], device_id=to, device_id_type=MESH
        )
        copy.start()
        started.append(copy)
        return copy

    mine = g_ref.at[:, y, z, x, c]
    here = handler == c
    away = jnp.logical_not(here)
    local = pltpu.make_async_copy(own_ref, mine, local_sem.at[5])

    def own_copy(dz, dy):
        return pltpu.make_async_remote_copy(
            src_ref=own_ref,
            dst_ref=mine,
            send_sem=send_sem.at[dz * parts + dy],
            recv_sem=recv_sem.at[dz * 4 + lax.rem(y, 2) * 2 + c],
            device_id={"rows_0": lax.rem(z + dz, deep), "cols": lax.rem(y + dy, parts), "rows_2": handler},
            device_id_type=MESH,
        )

    pl.when(here)(lambda: local.start())
    hops = [0] + [h for k in range(1, deep // 2) for h in (k, deep - k)] + [deep // 2]
    for dz in hops:
        for dy in range(parts):
            if dz == 0 and dy == 0:
                pl.when(away)(lambda: own_copy(0, 0).start())
            else:
                own_copy(dz, dy).start()
    pl.when(here)(lambda: local.wait())

    def pass_on(src, dst, by):
        i = slot[0]
        slot[0] += 1
        copy = pltpu.make_async_remote_copy(
            src_ref=src, dst_ref=dst, send_sem=send_sem.at[i], recv_sem=recv_sem.at[i],
            device_id={"cols": lax.rem(y + by + parts, parts)}, device_id_type=MESH,
        )
        copy.start()
        started.append(copy)
        return copy

    to_left = pass_on(own_int_ref, land_ref.at[0], -1)
    to_right = pass_on(own_int_ref, land_ref.at[2], 1)

    sibling = {"rows_2": 1 - c}
    pair = pl.ds(pl.multiple_of(2 * c, 2), 2)
    across = {k: [] for k in range(1, wide)}
    for dz in hops:
        at_z = lax.rem(z - dz + deep, deep)
        for p in range(2):
            for k in range(2):
                block = g_ref.at[:, 2 * c + p, at_z, x, k]
                copy = pltpu.make_async_remote_copy(
                    src_ref=block, dst_ref=block, send_sem=send_sem.at[0], recv_sem=recv_sem.at[dz * 4 + 2 * p + k],
                    device_id=sibling, device_id_type=MESH,
                )
                if dz == 0:
                    pl.when(jnp.logical_or(2 * c + p != y, c != k))(lambda copy=copy: copy.wait_recv())
                else:
                    copy.wait_recv()
        for dx in (1, wide - 1, 2):
            across[dx].append(send(g_ref.at[0, pair, at_z, x], {"rows_1": lax.rem(x + dx, wide)}))
    later = [(dx, send(g_ref.at[1, pair, :, x], {"rows_1": lax.rem(x + dx, wide)})) for dx in (1, wide - 1, 2)]

    swapped = [send(g_ref.at[0, pair, :, x], sibling)]
    for dx in (1, wide - 1, 2):
        for copy in across[dx]:
            copy.wait_recv()
        swapped.append(send(g_ref.at[0, pair, :, lax.rem(x - dx + wide, wide)], sibling))
    for copy in swapped:
        copy.wait_recv()
    swapped_later = []

    def swap_later():
        swapped_later.append(send(g_ref.at[1, pair, :, x], sibling))
        for dx, copy in later:
            copy.wait_recv()
            swapped_later.append(send(g_ref.at[1, pair, :, lax.rem(x - dx + wide, wide)], sibling))

    def end_swap():
        for copy in swapped_later:
            copy.wait_recv()

    onward, written = [], []

    def store(k):
        copy = pltpu.make_async_copy(land_ref.at[k], shard_ref.at[k], local_sem.at[8 + k])
        copy.start()
        written.append(copy)

    def relay():
        to_left.wait_recv()
        to_right.wait_recv()
        onward.append(pass_on(land_ref.at[2, 0], land_ref.at[1, 0], 1))
        onward.append(pass_on(land_ref.at[0, 1], land_ref.at[1, 1], -1))
        store(0)
        store(2)

    for copy in loads[2:]:
        copy.wait()

    def multiply(panel, step):
        if step % 2 == 0:
            at = pl.ds(PW * (step // 2), PW)
            prod_ref[panel, :, at] = nn(gt_ref[pl.ds(PW * panel, PW), :], all_v_ref[:, at], None)

    def write(panel):
        copy = pltpu.make_async_copy(prod_ref.at[panel], p_ref.at[panel], local_sem.at[6 + panel])
        copy.start()
        written.append(copy)

    factor_panels(
        slot_col, g_ref, gt_ref, l0_ref, l1_ref, ft_ref, i0_ref, i1_ref, a_ref, l_ref, tmp_ref, multiply, write, relay, swap_later, end_swap
    )
    for copy in onward:
        copy.wait_recv()
    store(1)
    for copy in written:
        copy.wait()

    for copy in started:
        copy.wait_send()
    for dz in hops:
        for dy in range(parts):
            if dz == 0 and dy == 0:
                pl.when(away)(lambda: own_copy(0, 0).wait_send())
            else:
                own_copy(dz, dy).wait_send()


def factor_panels(
    slot_col, g_ref, gt_ref, l0_ref, l1_ref, ft_ref, i0_ref, i1_ref, a_ref, l_ref, tmp_ref,
    multiply, write, relay, swap_later, end_swap,
):
    parts, deep, wide, cores, lines, cols = g_ref.shape[1:]
    rows = deep * wide * cores * lines
    depth = gt_ref.shape[1] // parts
    width = PW // parts

    def in_order(panel):
        at = pl.ds(PW * panel, PW)
        pick = (lax.broadcasted_iota(jnp.int32, (PW, rows), 1) == slot_col[panel]).astype(jnp.bfloat16)
        for y in range(parts):
            t = nn(pick, g_ref[panel, y].reshape(rows, cols), None)
            gt_ref[at, pl.ds(depth * y, depth)] = t[:, :depth].astype(jnp.bfloat16)
            i0_ref[at, pl.ds(width * y, width)] = t[:, depth : depth + width]
            if panel == 1:
                i1_ref[:, pl.ds(width * y, width)] = t[:, depth + width :]
        return gt_ref[at, :]

    def beside(step):
        multiply(0, step)
        if step == 16:
            swap_later()
        if step == 28:
            relay()

    g0 = in_order(0)
    own = i0_ref[pl.ds(0, PW), :]
    a_ref[...] = 0.5 * (own + own.T) - one_pass_nt(g0, g0)
    inverse_factor(a_ref, l_ref, tmp_ref, beside)
    write(0)
    end_swap()
    l0 = l_ref[...]
    high, low = split(l0)
    l0_ref[pl.ds(0, PW), :] = high
    l0_ref[pl.ds(PW, PW), :] = low
    g1 = in_order(1)
    g0 = gt_ref[pl.ds(0, PW), :]
    later = i0_ref[pl.ds(PW, PW), :] - one_pass_nt(g1, g0)
    ft = nt(later, l0).astype(jnp.bfloat16)
    ft_ref[...] = ft
    own = i1_ref[...]
    a_ref[...] = 0.5 * (own + own.T) - one_pass_nt(g1, g1) - one_pass_nt(ft, ft)

    def beside(step):
        multiply(1, step)

    inverse_factor(a_ref, l_ref, tmp_ref, beside)
    write(1)
    high, low = split(l_ref[...])
    l1_ref[pl.ds(0, PW), :] = high
    l1_ref[pl.ds(PW, PW), :] = low


def front(pivots, vectors, integrals):
    panels, width, columns = integrals.shape
    deep, wide, parts = lax.axis_size(ROWS[0]), lax.axis_size(ROWS[1]), lax.axis_size("cols")
    depth = vectors.shape[0]
    share = depth // parts
    across = share + panels * width
    full = jax.ShapeDtypeStruct
    bf, f32 = jnp.bfloat16, jnp.float32
    vmem, hbm = pl.BlockSpec(memory_space=pltpu.VMEM), pl.BlockSpec(memory_space=pl.ANY)
    copies = deep * parts + deep * (wide - 1) + 3 * wide + 3
    return pl.pallas_call(
        front_kernel,
        in_specs=[vmem, hbm, hbm],
        out_specs=[vmem, vmem, vmem, hbm, hbm],
        out_shape=(
            full((2 * PW, PW), bf),
            full((2 * PW, PW), bf),
            full((PW, PW), bf),
            full((parts - 1, *integrals.shape), bf),
            full((panels, PW, columns), f32),
        ),
        scratch_shapes=[
            pltpu.VMEM((2 * PW, depth), bf),
            pltpu.VMEM((depth, columns), bf),
            pltpu.VMEM((panels, PW, columns), f32),
            pltpu.VMEM(integrals.shape, bf),
            pltpu.VMEM((parts - 1, *integrals.shape), bf),
            pltpu.VMEM((panels, SLOTS, across), bf),
            pltpu.VMEM((panels, parts, deep, wide, 2, SLOTS, across), bf),
            pltpu.VMEM((2 * PW, PW), f32),
            pltpu.VMEM((PW, PW), f32),
            pltpu.VMEM((PW, PW), f32),
            pltpu.VMEM((PW, PW), f32),
            pltpu.VMEM((2, 16, 10, 8, 128), f32),
            pltpu.SemaphoreType.DMA((copies,)),
            pltpu.SemaphoreType.DMA((copies,)),
            pltpu.SemaphoreType.DMA((11,)),
        ],
        compiler_params=pltpu.CompilerParams(collective_id=0, has_side_effects=True, vmem_limit_bytes=56 << 20),
        cost_estimate=pl.CostEstimate(flops=2 * 10**9, bytes_accessed=40 << 20, transcendentals=0),
        name="front",
    )(pivots, vectors, integrals)


def apply_kernel(p_ref, own_ref, shard_ref, l0_ref, l1_ref, ft_ref, out_ref, r_ref, x_ref):
    me = lax.axis_index("cols")
    width = own_ref.shape[1]
    parts = shard_ref.shape[0] + 1
    for panel in range(PANELS):
        for k in range(parts):
            at = pl.ds(pl.multiple_of(lax.rem(me + k, parts) * width, width), width)
            shard = own_ref[panel] if k == 0 else shard_ref[k - 1, panel]
            r_ref[panel, at, :] = shard.astype(jnp.float32) - p_ref[panel, at, :]
    mine = pl.multiple_of(me * width, width)
    high, low = split(r_ref[0])
    both = nn(l0_ref[...], high, None)
    x = both[:PW] + both[PW:] + nn(l0_ref[pl.ds(0, PW), :], low, None)
    x_ref[...] = x
    out_ref[0] = x_ref[pl.ds(mine, width), :]
    turned = lax.dot_general(
        ft_ref[...], x.astype(jnp.bfloat16), (((1,), (0,)), ((), ())), preferred_element_type=jnp.float32
    )
    high, low = split(r_ref[1] - turned)
    lh = l1_ref[pl.ds(mine, width), :]
    ll = l1_ref[pl.ds(pl.multiple_of(PW + mine, width), width), :]
    out_ref[1] = nn(lh, high, None) + (nn(ll, high, None) + nn(lh, low, None))


def apply_factors(products, integrals, shards, l0, l1, ft):
    panels, width, columns = integrals.shape
    chunk = 1024
    whole = lambda x: pl.BlockSpec(x.shape, lambda j: (0,) * x.ndim, pipeline_mode=pl.Buffered(1))
    part = lambda *lead: pl.BlockSpec((*lead, chunk), lambda j: (0,) * len(lead) + (j,))
    return pl.pallas_call(
        apply_kernel,
        grid=(columns // chunk,),
        in_specs=[part(panels, PW), part(panels, width), part(shards.shape[0], panels, width)] + [whole(x) for x in (l0, l1, ft)],
        out_specs=part(panels, width),
        out_shape=jax.ShapeDtypeStruct((panels, width, columns), jnp.float32),
        scratch_shapes=[pltpu.VMEM((panels, PW, chunk), jnp.float32), pltpu.VMEM((PW, chunk), jnp.float32)],
        compiler_params=pltpu.CompilerParams(vmem_limit_bytes=60 << 20),
        cost_estimate=pl.CostEstimate(flops=3 * 10**9, bytes_accessed=16 << 20, transcendentals=0),
        name="apply",
    )(products, integrals, shards, l0, l1, ft)


def per_device(vectors, integrals, pivots):
    l0, l1, ft, shards, products = front(pivots, vectors, integrals)
    return apply_factors(products, integrals, shards, l0, l1, ft)


def solution(mesh):
    torus = Mesh(
        mesh.devices.reshape(8, 4, 2, mesh.shape["cols"]), ("rows_0", "rows_1", "rows_2", "cols")
    )
    return jax.shard_map(
        per_device,
        mesh=torus,
        in_specs=(P(None, ROWS), P(None, "cols", ROWS), P()),
        out_specs=P(None, "cols", ROWS),
        check_vma=False,
    )
```

```python
import functools

import jax
import jax.numpy as jnp
from jax import lax
from jax.experimental import pallas as pl
from jax.experimental.pallas import tpu as pltpu
from jax.sharding import Mesh
from jax.sharding import PartitionSpec as P

PW = 256
PANELS = 2
SLOTS = 8
ROWS = ("rows_0", "rows_1", "rows_2")
HI = lax.Precision.HIGHEST
MESH = pl.DeviceIdType.MESH
CHUNK = 1024


def total(terms):
    while len(terms) > 1:
        terms = [a + b for a, b in zip(terms[::2], terms[1::2])] + terms[len(terms) & ~1 :]
    return terms[0]


def bsub(x, k):
    return jnp.broadcast_to(x[k:k+1, :], (8, 128))

def blane(x, k):
    return jnp.broadcast_to(x[:, k:k+1], (8, 128))

def factor_inverse_128(rows, tmp_ref, meanwhile):
    sub = lax.broadcasted_iota(jnp.int32, (8, 128), 0)
    lane = lax.broadcasted_iota(jnp.int32, (8, 128), 1)
    out = []
    for s in range(16):
        meanwhile(s)
        base = 8 * s
        r = rows[s]
        cols = [blane(r, base + k) for k in range(8)]
        a = {}
        for k in range(8):
            tmp_ref[s, k] = cols[k]
        for k in range(8):
            for i in range(k, 8):
                a[i, k] = tmp_ref[s, k, pl.ds(i, 8, stride=0), :]
        unit, pivot = [], []
        for k in range(0, 8, 2):
            g = lambda i, j: a[max(i, j), min(i, j)]
            n = k + 1
            e, f, h = a[k, k], a[n, k], a[n, n]
            p = 1.0 / (e * h - f * f)
            t = f / e
            unit.append([g(k, j) for j in range(k)])
            unit.append([g(n, j) - t * g(k, j) for j in range(k)] + [t])
            pivot += [e, h - f * t]
            m = (h * p, -f * p, e * p)
            others = [i for i in range(8) if i not in (k, n)]
            w = {i: (g(i, k) * m[0] + g(i, n) * m[1], g(i, k) * m[1] + g(i, n) * m[2]) for i in others}
            new = dict(a)
            for x, i in enumerate(others):
                for j in others[: x + 1]:
                    new[i, j] = a[i, j] - (w[i][0] * g(j, k) + w[i][1] * g(j, n))
                new[max(i, k), min(i, k)] = w[i][0]
                new[max(i, n), min(i, n)] = w[i][1]
            new[k, k], new[n, k], new[n, n] = -m[0], -m[1], -m[2]
            a = new
        def column(vals):
            bit = 1
            while len(vals) > 1:
                vals = [jnp.where((sub & bit) > 0, b, a) for a, b in zip(vals[::2], vals[1::2])]
                bit *= 2
            return vals[0]
        g = lambda i, j: a[max(i, j), min(i, j)]
        ninv = [column([g(i, k) for i in range(8)]) for k in range(8)]
        scale = lax.rsqrt(column(pivot))
        kcol = []
        for j in range(8):
            v = jnp.where(sub == j, scale, 0.0)
            for i in range(j + 1, 8):
                v = jnp.where(sub == i, -unit[i][j] * scale, v)
            kcol.append(v)
        inblock = (lane >= base) & (lane < base + 8)
        rp = jnp.where(inblock, jnp.where(lane - base == sub, 1.0, 0.0), r)
        tmp_ref[s, 8] = rp
        brow = [tmp_ref[s, 8, pl.ds(k, 8, stride=0), :] for k in range(8)]
        fin = total([kcol[k] * brow[k] for k in range(8)])
        out.append(jnp.where(lane < base + 8, fin, 0.0))
        if s == 15:
            break
        ny = total([ninv[k] * brow[k] for k in range(8)])
        tmp_ref[s, 9] = ny
        yb = [tmp_ref[s, 9, pl.ds(k, 8, stride=0), :] for k in range(8)]
        for t in range(s + 1, 16):
            rt = rows[t]
            c = [blane(rt, base + k) for k in range(8)]
            acc = total([c[k] * yb[k] for k in range(8)])
            rows[t] = jnp.where(inblock, 0.0, rt) + acc
    return out

def nt(a, b, precision=HI):
    return lax.dot_general(a, b, (((1,), (1,)), ((), ())), precision=precision, preferred_element_type=jnp.float32)

def nn(a, b, precision=HI):
    return lax.dot_general(a, b, (((1,), (0,)), ((), ())), precision=precision, preferred_element_type=jnp.float32)

def inverse_factor(a_ref, l_ref, tmp_ref, meanwhile):
    half = lambda ref, r, c: ref[pl.ds(128 * r, 128), pl.ds(128 * c, 128)]
    w = factor_inverse_128([a_ref[pl.ds(8 * i, 8), pl.ds(0, 128)] for i in range(16)], tmp_ref.at[0], meanwhile)
    for i in range(16):
        l_ref[pl.ds(8 * i, 8), pl.ds(0, 128)] = w[i]
    l11 = half(l_ref, 0, 0)
    t21 = nt(half(a_ref, 1, 0), l11)
    a_ref[pl.ds(128, 128), pl.ds(128, 128)] = half(a_ref, 1, 1) - nt(t21, t21)
    w = factor_inverse_128([a_ref[pl.ds(128 + 8 * i, 8), pl.ds(128, 128)] for i in range(16)], tmp_ref.at[1], lambda s: meanwhile(16 + s))
    for i in range(16):
        l_ref[pl.ds(128 + 8 * i, 8), pl.ds(128, 128)] = w[i]
    l22 = half(l_ref, 1, 1)
    l_ref[pl.ds(128, 128), pl.ds(0, 128)] = -nn(l22, nn(t21, l11))
    l_ref[pl.ds(0, 128), pl.ds(128, 128)] = jnp.zeros((128, 128), jnp.float32)


def one_pass_nt(a, b):
    return nt(a, b, None)


def split(x):
    high = x.astype(jnp.bfloat16)
    return high, (x - high.astype(jnp.float32)).astype(jnp.bfloat16)


def place_pivots(pivot_ref, me, row_count):
    columns, places = [], []
    mine = me * SLOTS + lax.broadcasted_iota(jnp.int32, (SLOTS, PW), 0)
    for panel in range(PANELS):
        row = jnp.broadcast_to(pivot_ref[pl.ds(panel, 1), :], (PW, PW))
        col = row.T
        owner_row, owner_col = row // row_count, col // row_count
        same = owner_row == owner_col
        i = lax.broadcasted_iota(jnp.int32, (PW, PW), 0)
        j = lax.broadcasted_iota(jnp.int32, (PW, PW), 1)
        one = lambda mask: jnp.where(mask, 1, 0)
        rank_col = jnp.sum(one(same & (j < i)), axis=1, keepdims=True)
        rank_row = jnp.sum(one(same & (i < j)), axis=0, keepdims=True)
        columns.append(owner_col[:, :1] * SLOTS + rank_col)
        slot_row = owner_row[:1] * SLOTS + rank_row
        local = row[:1] - me * row_count + 1
        places.append(jnp.sum(jnp.where(slot_row == mine, local, 0), axis=1, keepdims=True) - 1)
    return columns, jnp.concatenate(places, axis=0)


def front_kernel(pivot_ref, v_ref, int_ref, out_ref,
                 l0_ref, l1_ref, ft_ref, gt_ref, all_v_ref, prod_ref, own_int_ref, land_ref, own_ref, g_ref, i0_ref, i1_ref, a_ref, l_ref, tmp_ref,
                 send_sem, recv_sem, local_sem):
    parts, deep, wide = g_ref.shape[1:4]
    z, x, c, y = (lax.axis_index(axis) for axis in (*ROWS, "cols"))
    handler = y // 2
    started = []
    depth = v_ref.shape[0] // parts
    width = int_ref.shape[1]
    row_count = v_ref.shape[1]

    barrier = pltpu.get_barrier_semaphore()

    def greet(**to):
        pl.semaphore_signal(barrier, device_id=to, device_id_type=MESH)

    for dz in range(deep):
        for p in range(2):
            for k in range(2):
                greet(rows_0=lax.rem(z + dz, deep), cols=2 * c + p, rows_2=k)
    for other in range(1, wide):
        greet(rows_1=lax.rem(x + other, wide))
    greet(cols=lax.rem(y + 1, parts))
    greet(cols=lax.rem(y + parts - 1, parts))
    greet(rows_2=1 - c)
    greeted = 4 * deep + wide + 2

    loads = [pltpu.make_async_copy(int_ref, own_int_ref, local_sem.at[0])]
    for k in range(parts):
        share = pl.ds(pl.multiple_of(lax.rem(y + k, parts) * depth, depth), depth)
        loads.append(pltpu.make_async_copy(v_ref.at[share], all_v_ref.at[share], local_sem.at[1 + k]))
    for copy in loads:
        copy.start()

    me = (z * wide + x) * 2 + c
    slot_col, place = place_pivots(pivot_ref, me, row_count)
    pick = (lax.broadcasted_iota(jnp.int32, (PANELS * SLOTS, row_count), 1) == place).astype(jnp.bfloat16)
    for copy in loads[:2]:
        copy.wait()
    share = all_v_ref[pl.ds(pl.multiple_of(y * depth, depth), depth), :]
    taken = one_pass_nt(pick, share).astype(jnp.bfloat16)
    own_ref[:, :, pl.ds(0, depth)] = taken.reshape(PANELS, SLOTS, depth)
    both = own_int_ref[...].reshape(PANELS * width, row_count)
    taken = one_pass_nt(pick, both).astype(jnp.bfloat16)
    own_ref[:, :, pl.ds(depth, PANELS * width)] = taken.reshape(PANELS, SLOTS, PANELS * width)
    pl.semaphore_wait(barrier, greeted)

    slot = [deep * parts]

    def send(part, to):
        i = slot[0]
        slot[0] += 1
        copy = pltpu.make_async_remote_copy(
            src_ref=part, dst_ref=part, send_sem=send_sem.at[i], recv_sem=recv_sem.at[i], device_id=to, device_id_type=MESH
        )
        copy.start()
        started.append(copy)
        return copy

    mine = g_ref.at[:, y, z, x, c]
    here = handler == c
    away = jnp.logical_not(here)
    local = pltpu.make_async_copy(own_ref, mine, local_sem.at[5])

    def own_copy(dz, dy):
        return pltpu.make_async_remote_copy(
            src_ref=own_ref,
            dst_ref=mine,
            send_sem=send_sem.at[dz * parts + dy],
            recv_sem=recv_sem.at[dz * 4 + lax.rem(y, 2) * 2 + c],
            device_id={"rows_0": lax.rem(z + dz, deep), "cols": lax.rem(y + dy, parts), "rows_2": handler},
            device_id_type=MESH,
        )

    pl.when(here)(lambda: local.start())
    hops = [0] + [h for k in range(1, deep // 2) for h in (k, deep - k)] + [deep // 2]
    for dz in hops:
        for dy in range(parts):
            if dz == 0 and dy == 0:
                pl.when(away)(lambda: own_copy(0, 0).start())
            else:
                own_copy(dz, dy).start()
    pl.when(here)(lambda: local.wait())

    def pass_on(src, dst, by):
        i = slot[0]
        slot[0] += 1
        copy = pltpu.make_async_remote_copy(
            src_ref=src, dst_ref=dst, send_sem=send_sem.at[i], recv_sem=recv_sem.at[i],
            device_id={"cols": lax.rem(y + by + parts, parts)}, device_id_type=MESH,
        )
        copy.start()
        started.append(copy)
        return copy

    to_left = pass_on(own_int_ref, land_ref.at[0], -1)
    to_right = pass_on(own_int_ref, land_ref.at[2], 1)

    sibling = {"rows_2": 1 - c}
    pair = pl.ds(pl.multiple_of(2 * c, 2), 2)
    across = {k: [] for k in range(1, wide)}
    for dz in hops:
        at_z = lax.rem(z - dz + deep, deep)
        for p in range(2):
            for k in range(2):
                block = g_ref.at[:, 2 * c + p, at_z, x, k]
                copy = pltpu.make_async_remote_copy(
                    src_ref=block, dst_ref=block, send_sem=send_sem.at[0], recv_sem=recv_sem.at[dz * 4 + 2 * p + k],
                    device_id=sibling, device_id_type=MESH,
                )
                if dz == 0:
                    pl.when(jnp.logical_or(2 * c + p != y, c != k))(lambda copy=copy: copy.wait_recv())
                else:
                    copy.wait_recv()
        for dx in (1, wide - 1, 2):
            across[dx].append(send(g_ref.at[0, pair, at_z, x], {"rows_1": lax.rem(x + dx, wide)}))
    later = [(dx, send(g_ref.at[1, pair, :, x], {"rows_1": lax.rem(x + dx, wide)})) for dx in (1, wide - 1, 2)]

    swapped = [send(g_ref.at[0, pair, :, x], sibling)]
    for dx in (1, wide - 1, 2):
        for copy in across[dx]:
            copy.wait_recv()
        swapped.append(send(g_ref.at[0, pair, :, lax.rem(x - dx + wide, wide)], sibling))
    for copy in swapped:
        copy.wait_recv()
    swapped_later = []

    def swap_later():
        swapped_later.append(send(g_ref.at[1, pair, :, x], sibling))
        for dx, copy in later:
            copy.wait_recv()
            swapped_later.append(send(g_ref.at[1, pair, :, lax.rem(x - dx + wide, wide)], sibling))

    def end_swap():
        for copy in swapped_later:
            copy.wait_recv()

    onward = []

    def relay():
        to_left.wait_recv()
        to_right.wait_recv()
        onward.append(pass_on(land_ref.at[2, 0], land_ref.at[1, 0], 1))
        onward.append(pass_on(land_ref.at[0, 1], land_ref.at[1, 1], -1))

    for copy in loads[2:]:
        copy.wait()

    def multiply(panel, step):
        if step % 2 == 0:
            at = pl.ds(PW * (step // 2), PW)
            prod_ref[panel, :, at] = nn(gt_ref[pl.ds(PW * panel, PW), :], all_v_ref[:, at], None)

    factor_panels(
        slot_col, g_ref, gt_ref, l0_ref, l1_ref, ft_ref, i0_ref, i1_ref, a_ref, l_ref, tmp_ref, multiply, relay, swap_later, end_swap
    )
    for copy in onward:
        copy.wait_recv()
    apply_factors(y, prod_ref, own_int_ref, land_ref, l0_ref, l1_ref, ft_ref, out_ref)

    for copy in started:
        copy.wait_send()
    for dz in hops:
        for dy in range(parts):
            if dz == 0 and dy == 0:
                pl.when(away)(lambda: own_copy(0, 0).wait_send())
            else:
                own_copy(dz, dy).wait_send()


def factor_panels(
    slot_col, g_ref, gt_ref, l0_ref, l1_ref, ft_ref, i0_ref, i1_ref, a_ref, l_ref, tmp_ref,
    multiply, relay, swap_later, end_swap,
):
    parts, deep, wide, cores, lines, cols = g_ref.shape[1:]
    rows = deep * wide * cores * lines
    depth = gt_ref.shape[1] // parts
    width = PW // parts

    def in_order(panel):
        at = pl.ds(PW * panel, PW)
        pick = (lax.broadcasted_iota(jnp.int32, (PW, rows), 1) == slot_col[panel]).astype(jnp.bfloat16)
        for y in range(parts):
            t = nn(pick, g_ref[panel, y].reshape(rows, cols), None)
            gt_ref[at, pl.ds(depth * y, depth)] = t[:, :depth].astype(jnp.bfloat16)
            i0_ref[at, pl.ds(width * y, width)] = t[:, depth : depth + width]
            if panel == 1:
                i1_ref[:, pl.ds(width * y, width)] = t[:, depth + width :]
        return gt_ref[at, :]

    def beside(step):
        multiply(0, step)
        if step == 16:
            swap_later()
        if step == 28:
            relay()

    g0 = in_order(0)
    own = i0_ref[pl.ds(0, PW), :]
    a_ref[...] = 0.5 * (own + own.T) - one_pass_nt(g0, g0)
    inverse_factor(a_ref, l_ref, tmp_ref, beside)
    end_swap()
    l0 = l_ref[...]
    high, low = split(l0)
    l0_ref[pl.ds(0, PW), :] = high
    l0_ref[pl.ds(PW, PW), :] = low
    g1 = in_order(1)
    g0 = gt_ref[pl.ds(0, PW), :]
    later = i0_ref[pl.ds(PW, PW), :] - one_pass_nt(g1, g0)
    ft = nt(later, l0).astype(jnp.bfloat16)
    ft_ref[...] = ft
    own = i1_ref[...]
    a_ref[...] = 0.5 * (own + own.T) - one_pass_nt(g1, g1) - one_pass_nt(ft, ft)

    def beside(step):
        multiply(1, step)

    inverse_factor(a_ref, l_ref, tmp_ref, beside)
    high, low = split(l_ref[...])
    l1_ref[pl.ds(0, PW), :] = high
    l1_ref[pl.ds(PW, PW), :] = low


def front(pivots, vectors, integrals):
    panels, width, columns = integrals.shape
    deep, wide, parts = lax.axis_size(ROWS[0]), lax.axis_size(ROWS[1]), lax.axis_size("cols")
    depth = vectors.shape[0]
    share = depth // parts
    across = share + panels * width
    full = jax.ShapeDtypeStruct
    bf, f32 = jnp.bfloat16, jnp.float32
    vmem, hbm = pl.BlockSpec(memory_space=pltpu.VMEM), pl.BlockSpec(memory_space=pl.ANY)
    copies = deep * parts + deep * (wide - 1) + 3 * wide + 3
    return pl.pallas_call(
        front_kernel,
        in_specs=[vmem, hbm, hbm],
        out_specs=vmem,
        out_shape=full((panels, width, columns), f32),
        scratch_shapes=[
            pltpu.VMEM((2 * PW, PW), bf),
            pltpu.VMEM((2 * PW, PW), bf),
            pltpu.VMEM((PW, PW), bf),
            pltpu.VMEM((2 * PW, depth), bf),
            pltpu.VMEM((depth, columns), bf),
            pltpu.VMEM((panels, PW, columns), f32),
            pltpu.VMEM(integrals.shape, bf),
            pltpu.VMEM((parts - 1, *integrals.shape), bf),
            pltpu.VMEM((panels, SLOTS, across), bf),
            pltpu.VMEM((panels, parts, deep, wide, 2, SLOTS, across), bf),
            pltpu.VMEM((2 * PW, PW), f32),
            pltpu.VMEM((PW, PW), f32),
            pltpu.VMEM((PW, PW), f32),
            pltpu.VMEM((PW, PW), f32),
            pltpu.VMEM((2, 16, 10, 8, 128), f32),
            pltpu.SemaphoreType.DMA((copies,)),
            pltpu.SemaphoreType.DMA((copies,)),
            pltpu.SemaphoreType.DMA((6,)),
        ],
        compiler_params=pltpu.CompilerParams(collective_id=0, has_side_effects=True, vmem_limit_bytes=56 << 20),
        cost_estimate=pl.CostEstimate(flops=2 * 10**9, bytes_accessed=40 << 20, transcendentals=0),
        name="front",
    )(pivots, vectors, integrals)


def apply_factors(me, r_ref, own_ref, shard_ref, l0_ref, l1_ref, ft_ref, out_ref):
    panels, width, columns = own_ref.shape
    parts = shard_ref.shape[0] + 1
    mine = pl.multiple_of(me * width, width)
    lh = l1_ref[pl.ds(mine, width), :]
    ll = l1_ref[pl.ds(pl.multiple_of(PW + mine, width), width), :]
    for start in range(0, columns, CHUNK):
        cols = pl.ds(start, CHUNK)
        for panel in range(panels):
            for k in range(parts):
                at = pl.ds(pl.multiple_of(lax.rem(me + k, parts) * width, width), width)
                shard = own_ref[panel, :, cols] if k == 0 else shard_ref[k - 1, panel, :, cols]
                r_ref[panel, at, cols] = shard.astype(jnp.float32) - r_ref[panel, at, cols]
        high, low = split(r_ref[0, :, cols])
        both = nn(l0_ref[...], high, None)
        x = both[:PW] + both[PW:] + nn(l0_ref[pl.ds(0, PW), :], low, None)
        r_ref[0, :, cols] = x
        out_ref[0, :, cols] = r_ref[0, pl.ds(mine, width), cols]
        turned = lax.dot_general(
            ft_ref[...], x.astype(jnp.bfloat16), (((1,), (0,)), ((), ())), preferred_element_type=jnp.float32
        )
        high, low = split(r_ref[1, :, cols] - turned)
        out_ref[1, :, cols] = nn(lh, high, None) + (nn(ll, high, None) + nn(lh, low, None))


def per_device(vectors, integrals, pivots):
    return front(pivots, vectors, integrals)


def solution(mesh):
    torus = Mesh(
        mesh.devices.reshape(8, 4, 2, mesh.shape["cols"]), ("rows_0", "rows_1", "rows_2", "cols")
    )
    return jax.shard_map(
        per_device,
        mesh=torus,
        in_specs=(P(None, ROWS), P(None, "cols", ROWS), P()),
        out_specs=P(None, "cols", ROWS),
        check_vma=False,
    )
```
